32 devices in a mesh: seq: 8 (over z, y), mlp: 4 (over x, core).
Axes of the slice: x: 2, y: 2, z: 4, core: 2. Of those that a mesh axis runs over, the one named last changes fastest.
Arguments:
- block_input: bfloat16 [8, 512, 2048], P('mlp', 'seq'), may hold values from -6 to 6
- w_branch: bfloat16 [2048, 2560], P(('seq', 'mlp')), may hold values from -0.125 to 0.125
- w_recur_in: bfloat16 [2048, 2560], P(('seq', 'mlp')), may hold values from -0.125 to 0.125
- w_recur_out: bfloat16 [2560, 2048], P(('seq', 'mlp')), may hold values from -0.25 to 0.25
- w_rgate: bfloat16 [2560, 256], P(('seq', 'mlp')), may hold values from -0.375 to 0.375
- w_igate: bfloat16 [2560, 256], P(('seq', 'mlp')), may hold values from -0.375 to 0.375
- conv_weight: bfloat16 [4, 2560], P(None, ('seq', 'mlp')), may hold values from -3 to 3
- conv_bias: bfloat16 [2560], P(('seq', 'mlp')), may hold values from -3 to 3
- rgate_bias: bfloat16 [2560], P(('seq', 'mlp')), may hold values from -3 to 3
- igate_bias: bfloat16 [2560], P(('seq', 'mlp')), may hold values from -3 to 3
- rate_param: bfloat16 [2560], P(('seq', 'mlp')), may hold values from -15 to -3
- norm_gain: bfloat16 [2048], P(('seq', 'mlp')), may hold values from 0.25 to 1.75
- mlp_gain: bfloat16 [2048], P(('seq', 'mlp')), may hold values from 0.25 to 1.75
- w_gate: bfloat16 [2048, 6144], P('seq', 'mlp'), may hold values from -0.125 to 0.125
- w_up: bfloat16 [2048, 6144], P('seq', 'mlp'), may hold values from -0.125 to 0.125
- w_down: bfloat16 [6144, 2048], P('mlp', 'seq'), may hold values from -0.15625 to 0.15625
- cotangent: bfloat16 [8, 512, 2048], P('mlp', 'seq'), may hold values from -6 to 6
Outputs:
- block_output: bfloat16 [8, 512, 2048], P('mlp', 'seq')
- input_grad: bfloat16 [8, 512, 2048], P('mlp', 'seq')
- grad_branch: float32 [2048, 2560], P(('seq', 'mlp'))
- grad_recur_in: float32 [2048, 2560], P(('seq', 'mlp'))
- grad_recur_out: float32 [2560, 2048], P(('seq', 'mlp'))
- grad_rgate: float32 [2560, 256], P(('seq', 'mlp'))
- grad_igate: float32 [2560, 256], P(('seq', 'mlp'))
- grad_conv_weight: float32 [4, 2560], P(None, ('seq', 'mlp'))
- grad_conv_bias: float32 [2560], P(('seq', 'mlp'))
- grad_rgate_bias: float32 [2560], P(('seq', 'mlp'))
- grad_igate_bias: float32 [2560], P(('seq', 'mlp'))
- grad_rate: float32 [2560], P(('seq', 'mlp'))
- grad_norm_gain: float32 [2048], P(('seq', 'mlp'))
- grad_mlp_gain: float32 [2048], P(('seq', 'mlp'))
- grad_gate: float32 [2048, 6144], P('seq', 'mlp')
- grad_up: float32 [2048, 6144], P('seq', 'mlp')
- grad_down: float32 [6144, 2048], P('mlp', 'seq')
The draws below stay inside these ranges and needn't reach their ends.
All inputs are finite; a program needn't handle non-finite values.
Results may differ from the reference program's by a relative error of at most 0.013.
Values may be sent and summed in bfloat16 or wider, within the bound.
No kernel may reach another device: no remote copies, remote signals or barrier semaphores. Data moves between devices by JAX's collectives and lax.ppermute only.
A program may use at most 256 MiB of HBM per device.

```python
import jax
import jax.numpy as jnp
from jax import lax

D = 2048
R = 2560
FF = 6144
HEADS = 10
CONV = 4
BW = 256
SEQS = 8
LEN = 512


def draw_rate_param(key, part):
    key_slow, key_fast, key_pick = jax.random.split(key, 3)
    slow_rates = jnp.exp(jax.random.uniform(key_slow, (R,), jnp.float32, jnp.log(0.02 / LEN), jnp.log(0.2 / LEN)))
    fast_rates = jnp.exp(jax.random.uniform(key_fast, (R,), jnp.float32, jnp.log(2.0 / LEN), jnp.log(0.03)))
    fast_share = 0.5
    chosen = jnp.where(jax.random.uniform(key_pick, (R,), jnp.float32) < fast_share, fast_rates, slow_rates)
    return jnp.log(jnp.expm1(chosen)).astype(jnp.bfloat16)


def levels(rng, dims, cuts, least, largest):
    level = 1.0
    for dim, blocks in cuts:
        steps = jax.random.uniform(jax.random.fold_in(jax.random.fold_in(rng, 6), dim), (blocks,), jnp.float32, least / len(cuts), largest / len(cuts))
        level = level * jnp.repeat(jnp.exp(steps), dims[dim] // blocks).reshape((-1,) + (1,) * (len(dims) - 1 - dim))
    return level


def noise(stream_key, dims, width, reach, pieces=(), held_as=jnp.bfloat16):
    array = width * jax.random.normal(stream_key, dims, jnp.float32)
    if pieces:
        array = array * levels(stream_key, dims, pieces, -0.22, 0.18)
    return jnp.clip(array, -reach, reach).astype(held_as)


def setup_inputs(seed: int = 0) -> dict:
    key_list = jax.random.split(jax.random.key(seed), 18)
    return {
        "block_input": noise(key_list[0], (SEQS, LEN, D), 1.0, 6.0, ((0, 4), (1, 8))),
        "w_branch": noise(key_list[1], (D, R), D ** -0.5, 0.125, ((0, 32),)),
        "w_recur_in": noise(key_list[2], (D, R), D ** -0.5, 0.125, ((0, 32),)),
        "w_recur_out": noise(key_list[3], (R, D), (R // 4) ** -0.5, 0.25, ((0, 32),)),
        "w_rgate": noise(key_list[4], (R, BW), BW ** -0.5, 0.375, ((0, 32),)),
        "w_igate": noise(key_list[5], (R, BW), BW ** -0.5, 0.375, ((0, 32),)),
        "conv_weight": noise(key_list[6], (CONV, R), CONV ** -0.5, 3.0, ((1, 32),)),
        "conv_bias": noise(key_list[7], (R,), 0.5, 3.0, ((0, 32),)),
        "rgate_bias": noise(key_list[8], (R,), 0.5, 3.0, ((0, 32),)),
        "igate_bias": noise(key_list[9], (R,), 0.5, 3.0, ((0, 32),)),
        "rate_param": draw_rate_param(jax.random.fold_in(key_list[17], 71), 0),
        "norm_gain": jnp.clip(1.0 + 0.15 * jax.random.normal(key_list[11], (D,), jnp.float32), 0.25, 1.75).astype(jnp.bfloat16),
        "mlp_gain": jnp.clip(1.0 + 0.15 * jax.random.normal(key_list[12], (D,), jnp.float32), 0.25, 1.75).astype(jnp.bfloat16),
        "w_gate": noise(key_list[13], (D, FF), D ** -0.5, 0.125, ((0, 8), (1, 4))),
        "w_up": noise(key_list[14], (D, FF), D ** -0.5, 0.125, ((0, 8), (1, 4))),
        "w_down": noise(key_list[15], (FF, D), (FF // 4) ** -0.5, 0.15625, ((0, 4), (1, 8))),
        "cotangent": noise(key_list[16], (SEQS, LEN, D), 1.0, 6.0, ((0, 4), (1, 8))),
    }


@jax.custom_vjp
def low(v):
    return lax.optimization_barrier(v.astype(jnp.bfloat16)).astype(jnp.float32)

@jax.custom_vjp
def low_back(v):
    return v

def low_keep(v):
    return (low(v), None)

def low_pass(kept, grad):
    return (grad,)

def back_keep(v):
    return (v, None)

def back_low(kept, grad):
    return (low(grad),)
low.defvjp(low_keep, low_pass)
low_back.defvjp(back_keep, back_low)

def product(left, right):
    return jnp.dot(left, right, precision=lax.Precision.HIGHEST, preferred_element_type=jnp.float32)

def rms_scale(values, gain):
    return values * lax.rsqrt(lax.optimization_barrier(jnp.mean(values * values, axis=-1, keepdims=True)) + 1e-06) * gain

def head_mix(values, weight):
    length = values.shape[0]
    block_width = weight.shape[1]
    mixed_heads = jnp.einsum('thj,hjk->thk', values.reshape(length, HEADS, block_width), weight.reshape(HEADS, block_width, block_width), precision=lax.Precision.HIGHEST)
    return mixed_heads.reshape(length, HEADS * block_width)

def one_sequence(params, seq_rows):
    w_branch, w_recur_in, w_recur_out, w_rgate, w_igate, conv_weight, conv_bias, rgate_bias, igate_bias, rate_param, norm_gain, mlp_gain, w_gate, w_up, w_down = params
    length = seq_rows.shape[0]
    normed = low(rms_scale(seq_rows, norm_gain))
    branch_pre = low_back(product(normed, w_branch))
    branch_act = jax.nn.gelu(branch_pre, approximate=True)
    recur_pre = low_back(product(normed, w_recur_in))
    padded = jnp.concatenate([jnp.zeros((CONV - 1, recur_pre.shape[1]), jnp.float32), recur_pre], axis=0)
    conv_out = conv_bias + sum((conv_weight[k] * padded[CONV - 1 - k:CONV - 1 - k + length] for k in range(CONV)))
    conv_low = low(conv_out)
    r_pre = low_back(head_mix(conv_low, w_rgate) + rgate_bias)
    i_pre = low_back(head_mix(conv_low, w_igate) + igate_bias)
    decay_log = -8.0 * jax.nn.softplus(rate_param) * jax.nn.sigmoid(r_pre)
    decay_rate = jnp.exp(decay_log)
    driven = jax.nn.sigmoid(i_pre) * conv_out * jnp.sqrt(-jnp.expm1(2.0 * decay_log))

    def advance(carry_state, step_pair):
        carry_state = step_pair[0] * carry_state + step_pair[1]
        return (carry_state, carry_state)
    _, states = lax.scan(advance, jnp.zeros((recur_pre.shape[1],), jnp.float32), (decay_rate, driven))
    mixed_out = low(states * branch_act)
    recur_out = low_back(product(mixed_out, w_recur_out))
    middle = seq_rows + recur_out
    normed2 = low(rms_scale(middle, mlp_gain))
    gate_pre = low_back(product(normed2, w_gate))
    up_pre = low_back(product(normed2, w_up))
    hidden = low(jax.nn.gelu(gate_pre, approximate=True) * up_pre)
    return middle + product(hidden, w_down)

def reference(block_input, w_branch, w_recur_in, w_recur_out, w_rgate, w_igate, conv_weight, conv_bias, rgate_bias, igate_bias, rate_param, norm_gain, mlp_gain, w_gate, w_up, w_down, cotangent):
    params = (w_branch.astype(jnp.float32), w_recur_in.astype(jnp.float32), w_recur_out.astype(jnp.float32), w_rgate.astype(jnp.float32), w_igate.astype(jnp.float32), conv_weight.astype(jnp.float32), conv_bias.astype(jnp.float32), rgate_bias.astype(jnp.float32), igate_bias.astype(jnp.float32), rate_param.astype(jnp.float32), norm_gain.astype(jnp.float32), mlp_gain.astype(jnp.float32), w_gate.astype(jnp.float32), w_up.astype(jnp.float32), w_down.astype(jnp.float32))

    def forward(inputs, weights):
        return lax.map(jax.checkpoint(lambda seq_rows: one_sequence(weights, seq_rows)), inputs)
    block_out, pullback = jax.vjp(forward, block_input.astype(jnp.float32), params)
    grad_in, grads = pullback(cotangent.astype(jnp.float32))
    return (block_out.astype(jnp.bfloat16), grad_in.astype(jnp.bfloat16), grads[0], grads[1], grads[2], grads[3], grads[4], grads[5], grads[6], grads[7], grads[8], grads[9], grads[10], grads[11], grads[12], grads[13], grads[14])
```

```python
from functools import partial

import jax
import jax.numpy as jnp
from jax import lax
from jax.experimental import pallas as pl
from jax.experimental.pallas import tpu as pltpu
from jax.sharding import Mesh, PartitionSpec as P

HEADS = 10
CONV = 4
RING = (0, 1, 3, 2)
F32 = jnp.float32
BF16 = jnp.bfloat16
PAIR = ((0, 1), (1, 0))


def swap(value, axis):
    return lax.ppermute(value, axis, PAIR)


def low(value):
    return value.astype(BF16)


def ordered(first, mine, theirs, axis):
    return jnp.where(
        first, jnp.concatenate([mine, theirs], axis), jnp.concatenate([theirs, mine], axis)
    )


def pick(array, index, axis):
    return lax.dynamic_index_in_dim(array, index, axis, keepdims=False)


def z_ring():
    return lax.axis_size("z") == len(RING)


def z_at(j):
    if not z_ring():
        return jnp.int32(j)
    here = pick(jnp.array(RING, jnp.int32), lax.axis_index("z"), 0)
    return pick(jnp.array(RING, jnp.int32), (here - j) % len(RING), 0)


def z_place(z):
    if not z_ring():
        return jnp.int32(z)
    table = jnp.array(RING, jnp.int32)
    return (pick(table, lax.axis_index("z"), 0) - RING[z]) % len(RING)


def z_next(value):
    count = len(RING)
    return lax.ppermute(value, "z", [(RING[p], RING[(p + 1) % count]) for p in range(count)])


def z_gather(shard):
    if not z_ring():
        everything = lax.all_gather(shard, "z")
        return [everything[j] for j in range(lax.axis_size("z"))]
    shards = [shard]
    for _ in range(len(RING) - 1):
        shards.append(z_next(shards[-1]))
    return shards


def z_scatter(part):
    count = lax.axis_size("z")
    if not z_ring():
        stacked = jnp.stack([low(part(j)) for j in range(count)])
        return lax.psum_scatter(stacked, "z", scatter_dimension=0).astype(F32)
    total = None
    for j in list(range(1, count)) + [0]:
        term = part(j)
        if total is not None:
            term = term + total.astype(F32)
        total = z_next(low(term)) if j else term
    return total


def z_shift(value, steps):
    count = lax.axis_size("z")
    return lax.ppermute(
        value, "z", [(s, s + steps) for s in range(count) if 0 <= s + steps < count]
    )


def z_carry(decay, state, step):
    count = lax.axis_size("z")
    pair = jnp.stack([decay, state])
    if z_ring():
        near = [z_shift(pair, step * k) for k in range(1, count)]
        carry = near[-1][1]
        for got in near[-2::-1]:
            carry = got[1] + got[0] * carry
        return carry
    everything, here = lax.all_gather(pair, "z"), lax.axis_index("z")

    def hop(k, before):
        at = k if step == 1 else count - 1 - k
        reached = at < here if step == 1 else at > here
        return jnp.where(reached, everything[at, 1] + everything[at, 0] * before, before)

    return lax.fori_loop(0, count, hop, jnp.zeros_like(state))


def group_gather(own):
    half = own.shape[0] // 2
    over_x, over_y = swap(own, "x"), swap(own, "y")
    corner = jnp.concatenate([swap(over_x[:half], "y"), swap(over_y[half:], "x")])
    near = jnp.concatenate([over_x, over_y, corner])
    return jnp.concatenate([own, near, swap(own, "c"), swap(near, "c")])


def group_scatter(partial_sum):
    rows = partial_sum.shape[0] // 8
    mine = partial_sum[: 4 * rows] + swap(low(partial_sum[4 * rows :]), "c").astype(F32)
    own, to_x, to_y, corner = (mine[k * rows : (k + 1) * rows] for k in range(4))
    half = rows // 2
    via_x = swap(low(corner[:half]), "x").astype(F32)
    via_y = swap(low(corner[half:]), "y").astype(F32)
    to_y = jnp.concatenate([to_y[:half] + via_x, to_y[half:]])
    to_x = jnp.concatenate([to_x[:half], to_x[half:] + via_y])
    return own + swap(low(to_x), "x").astype(F32) + swap(low(to_y), "y").astype(F32)


def fine_gather(shard, first, second):
    shards = z_gather(shard)
    near = [swap(s, first) for s in shards]
    far = [swap(s, second) for s in shards]
    both = [swap(s, second) for s in near]
    over_y, over_x = (near, far) if first == "y" else (far, near)
    return jnp.concatenate(shards + over_y + over_x + both)


def fine_scatter(full, first, second):
    count = lax.axis_size("z")
    blocks = full.reshape((2, 2, count, -1) + full.shape[1:])

    def part(j):
        def block(on_first, on_second):
            over_x, over_y = (on_second, on_first) if second == "x" else (on_first, on_second)
            return blocks[over_x, over_y, j]

        sent = swap(low(block(1, 1)), second).astype(F32)
        near = swap(low(block(1, 0) + sent), first).astype(F32)
        return block(0, 0) + swap(low(block(0, 1)), second).astype(F32) + near

    return z_scatter(part)


def fine_chips():
    y, x = lax.axis_index("y"), lax.axis_index("x")
    count = lax.axis_size("z")
    return [
        (z_at(j) * 2 + (y ^ over_y)) * 2 + (x ^ over_x)
        for over_x in (0, 1)
        for over_y in (0, 1)
        for j in range(count)
    ]


def fine_places():
    y, x = lax.axis_index("y"), lax.axis_index("x")
    count = lax.axis_size("z")
    return [
        ((x ^ at_x) * 2 + (y ^ at_y)) * count + z_place(z)
        for z in range(count)
        for at_y in (0, 1)
        for at_x in (0, 1)
    ]


def columns(values, places):
    width = values.shape[-1] // len(places)
    return jnp.concatenate(
        [lax.dynamic_slice_in_dim(values, at * width, width, values.ndim - 1) for at in places],
        axis=-1,
    )


def whole_gather(shard, first, second):
    shards = jnp.stack(z_gather(shard))
    count = lax.axis_size("z")
    if z_ring():
        shards = jnp.stack([pick(shards, z_place(z), 0) for z in range(count)])
    at = {"y": lax.axis_index("y"), "x": lax.axis_index("x")}
    near = swap(shards, first)
    held = jnp.stack([shards, near], 1)
    far = swap(held, second)
    both = jnp.where(at[first] == 0, held, held[:, ::-1])
    far = jnp.where(at[first] == 0, far, far[:, ::-1])
    full = jnp.where(at[second] == 0, jnp.stack([both, far], 2), jnp.stack([far, both], 2))
    if first == "x":
        full = jnp.swapaxes(full, 1, 2)
    return full.reshape((-1,) + shard.shape[1:])


def whole_scatter(full, first, second):
    count = lax.axis_size("z")
    blocks = full.reshape((count, 2, 2, -1) + full.shape[1:])
    places = {"y": 1, "x": 2}
    for axis in (second, first):
        at, dim = lax.axis_index(axis), places.pop(axis)
        dim = min(dim, blocks.ndim - full.ndim - 1)
        sent = swap(low(pick(blocks, 1 - at, dim)), axis)
        blocks = pick(blocks, at, dim) + sent.astype(F32)
    return z_scatter(lambda j: pick(blocks, z_at(j), 0))


def to_halves(count):
    return [(count // 2 * c + q, 2 * q + c) for q in range(count // 2) for c in range(2)]


EVERY = ("z", "y", "x", "c")


def expm1_neg(value):
    series = 1.0
    for k in range(10, 1, -1):
        series = 1.0 + value / k * series
    return jnp.where(value > -1.0, -value * series, 1.0 - jnp.exp(value))


def forward_kernel(
    rec_ref, halo_ref, vec_ref, wr_ref, wi_ref, conv_ref, sr_ref, si_ref, a_ref, s_ref, p_ref, ext
):
    head, heads = pl.program_id(0), pl.num_programs(0)
    seqs, length, width = rec_ref.shape
    lanes = pl.ds(pl.multiple_of(head * width, width), width)
    vec = vec_ref[...]
    for s in range(seqs):
        ext[s, 0:8, :] = halo_ref[s]
        ext[s, 8 : 8 + length, :] = rec_ref[s]
        conv = vec[4:5] + sum(
            vec[k : k + 1] * ext[s, 8 - k : 8 - k + length, :] for k in range(CONV)
        )
        conv_low = low(conv)
        sig_r = jax.nn.sigmoid(
            jnp.dot(conv_low, wr_ref[...], preferred_element_type=F32) + vec[5:6]
        )
        sig_i = jax.nn.sigmoid(
            jnp.dot(conv_low, wi_ref[...], preferred_element_type=F32) + vec[6:7]
        )
        decay_log = vec[7:8] * sig_r
        conv_ref[s] = conv
        sr_ref[s] = sig_r
        si_ref[s] = sig_i
        a_ref[s, :, lanes] = jnp.exp(decay_log)
        s_ref[s, :, lanes] = sig_i * conv * jnp.sqrt(expm1_neg(2.0 * decay_log))

    @pl.when(head == heads - 1)
    def _():
        def step(t, carry):
            new = []
            for s in range(seqs):
                prod, state = carry[s]
                row = pl.ds(t, 1)
                decay = a_ref[s, row, :]
                prod = decay * prod
                state = decay * state + s_ref[s, row, :]
                p_ref[s, row, :] = prod
                s_ref[s, row, :] = state
                new.append((prod, state))
            return tuple(new)

        full = a_ref.shape[2]
        start = (jnp.ones((1, full), F32), jnp.zeros((1, full), F32))
        lax.fori_loop(0, length, step, (start,) * seqs)


def reverse_kernel(a_ref, g_ref, l_ref, q_ref, e_ref):
    seqs, length, full = a_ref.shape

    def step(k, carry):
        t = length - 1 - k
        new = []
        for s in range(seqs):
            prod, sent = carry[s]
            row = pl.ds(t, 1)
            q_ref[s, row, :] = prod
            delta = g_ref[s, row, :] + sent
            l_ref[s, row, :] = delta
            decay = a_ref[s, row, :]
            new.append((prod * decay, decay * delta))
        return tuple(new)

    start = (jnp.ones((1, full), F32), jnp.zeros((1, full), F32))
    last = lax.fori_loop(0, length, step, (start,) * seqs)
    for s in range(seqs):
        e_ref[pl.ds(s, 1), :] = last[s][1]


def backward_kernel(
    l_ref, q_ref, e_ref, s_ref, p_ref, carry_ref, conv_ref, sr_ref, si_ref, rec_ref, halo_ref,
    vec_ref, wr_ref, wi_ref, gconv_ref, gwr_ref, gwi_ref, small_ref, ext, before,
):
    seqs, length, width = rec_ref.shape
    vec = vec_ref[...]
    rows = [jnp.zeros((1, width), F32)] * 8
    contract_rows = (((0,), (0,)), ((), ()))
    contract_last = (((1,), (1,)), ((), ()))
    for s in range(seqs):
        ext[s, 0:8, :] = halo_ref[s]
        ext[s, 8 : 8 + length, :] = rec_ref[s]
        carry = carry_ref[s : s + 1, :]
        before[s, 0:8, :] = jnp.broadcast_to(carry, (8, width))
        before[s, 8 : 8 + length, :] = s_ref[s] + p_ref[s] * carry
        prev = before[s, 7 : 7 + length, :]
        delta = l_ref[s] + q_ref[s] * e_ref[s : s + 1, :]
        conv, sig_r, sig_i = conv_ref[s], sr_ref[s], si_ref[s]
        decay_log = vec[7:8] * sig_r
        decay = jnp.exp(decay_log)
        scale = jnp.sqrt(expm1_neg(2.0 * decay_log))
        through = delta * sig_i
        grad_log = delta * prev * decay - through * conv * decay * decay / scale
        slope_r = grad_log * sig_r
        rows[7] = rows[7] + jnp.sum(slope_r, axis=0, keepdims=True)
        grad_r = low(slope_r * vec[7:8] * (1.0 - sig_r))
        grad_i = low(through * conv * scale * (1.0 - sig_i))
        conv_low = low(conv)
        gwr = lax.dot_general(conv_low, grad_r, contract_rows, preferred_element_type=F32)
        gwi = lax.dot_general(conv_low, grad_i, contract_rows, preferred_element_type=F32)
        if s == 0:
            gwr_ref[...], gwi_ref[...] = gwr, gwi
        else:
            gwr_ref[...] += gwr
            gwi_ref[...] += gwi
        rows[5] = rows[5] + jnp.sum(grad_r.astype(F32), axis=0, keepdims=True)
        rows[6] = rows[6] + jnp.sum(grad_i.astype(F32), axis=0, keepdims=True)
        grad_conv = (
            through * scale
            + lax.dot_general(grad_r, wr_ref[...], contract_last, preferred_element_type=F32)
            + lax.dot_general(grad_i, wi_ref[...], contract_last, preferred_element_type=F32)
        )
        gconv_ref[s] = grad_conv
        rows[4] = rows[4] + jnp.sum(grad_conv, axis=0, keepdims=True)
        for k in range(CONV):
            tap = grad_conv * ext[s, 8 - k : 8 - k + length, :]
            rows[k] = rows[k] + jnp.sum(tap, axis=0, keepdims=True)
    for k in range(8):
        small_ref[k : k + 1, :] = rows[k]


def cost(flops, values):
    return pl.CostEstimate(flops=flops, bytes_accessed=values, transcendentals=0)


def run_forward(rec, halo, vec, gates):
    seqs, length, full = rec.shape
    heads = HEADS // 2
    width = full // heads
    block = pl.BlockSpec((seqs, length, width), lambda h: (0, 0, h))
    whole = pl.BlockSpec((seqs, length, full), lambda h: (0, 0, 0))
    array = jax.ShapeDtypeStruct(rec.shape, F32)
    return pl.pallas_call(
        forward_kernel,
        grid=(heads,),
        in_specs=[
            block,
            pl.BlockSpec((seqs, 8, width), lambda h: (0, 0, h)),
            pl.BlockSpec((8, width), lambda h: (0, h)),
            pl.BlockSpec((width, width), lambda h: (h, 0)),
            pl.BlockSpec((width, width), lambda h: (h, 1)),
        ],
        out_specs=[block, block, block, whole, whole, whole],
        out_shape=[array] * 6,
        scratch_shapes=[pltpu.VMEM((seqs, length + 8, width), F32)],
        cost_estimate=cost(seqs * length * full * width * 4, rec.size * 28),
        name="recur_forward",
    )(rec, halo, vec, gates, gates)


def run_reverse(decay, grad_states):
    seqs, length, full = decay.shape
    array = jax.ShapeDtypeStruct(decay.shape, F32)
    return pl.pallas_call(
        reverse_kernel,
        out_shape=[array, array, jax.ShapeDtypeStruct((seqs, full), F32)],
        cost_estimate=cost(decay.size * 4, decay.size * 16),
        name="recur_reverse",
    )(decay, grad_states)


def run_backward(local, ahead, entering, state, prod, carry, conv, sig_r, sig_i, rec, halo, vec, gates):
    seqs, length, full = rec.shape
    heads = HEADS // 2
    width = full // heads
    block = pl.BlockSpec((seqs, length, width), lambda h: (0, 0, h))
    row = pl.BlockSpec((seqs, width), lambda h: (0, h))
    weight = pl.BlockSpec((width, width), lambda h: (h, 0))
    return pl.pallas_call(
        backward_kernel,
        grid=(heads,),
        in_specs=[
            block,
            block,
            row,
            block,
            block,
            row,
            block,
            block,
            block,
            block,
            pl.BlockSpec((seqs, 8, width), lambda h: (0, 0, h)),
            pl.BlockSpec((8, width), lambda h: (0, h)),
            weight,
            pl.BlockSpec((width, width), lambda h: (h, 1)),
        ],
        out_specs=[block, weight, weight, pl.BlockSpec((8, width), lambda h: (0, h))],
        out_shape=[
            jax.ShapeDtypeStruct(rec.shape, F32),
            jax.ShapeDtypeStruct((full, width), F32),
            jax.ShapeDtypeStruct((full, width), F32),
            jax.ShapeDtypeStruct((8, full), F32),
        ],
        scratch_shapes=[pltpu.VMEM((seqs, length + 8, width), F32)] * 2,
        cost_estimate=cost(seqs * length * full * width * 8, rec.size * 40),
        name="recur_backward",
    )(local, ahead, entering, state, prod, carry, conv, sig_r, sig_i, rec, halo, vec, gates, gates)


def rms_scale(values, gain):
    return values * lax.rsqrt(jnp.mean(values * values, axis=-1, keepdims=True) + 1e-06) * gain


def mlp_act(gate_pre, up_pre):
    return jax.nn.gelu(gate_pre, approximate=True) * up_pre


def mm(left, right):
    return jnp.dot(left, right, preferred_element_type=F32)


def mm_rows(left, weight):
    return lax.dot_general(left, weight, (((1,), (1,)), ((), ())), preferred_element_type=F32)


def outer_sum(left, right):
    return lax.dot_general(left, right, (((0,), (0,)), ((), ())), preferred_element_type=F32)


def on_device(
    block_input,
    w_branch,
    w_recur_in,
    w_recur_out,
    w_rgate,
    w_igate,
    conv_weight,
    conv_bias,
    rgate_bias,
    igate_bias,
    rate_param,
    norm_gain,
    mlp_gain,
    w_gate,
    w_up,
    w_down,
    cotangent,
):
    z, y, c = (lax.axis_index(axis) for axis in ("z", "y", "c"))
    z_count = lax.axis_size("z")
    devices = z_count * 8
    first_y, first_c = y == 0, c == 0
    half_tokens, width = block_input.shape[1:]
    length = 2 * half_tokens
    channels = w_branch.shape[1] // 2
    z_places = [z_at(j) for j in range(z_count)]
    z_back = [z_place(j) for j in range(z_count)]

    def own_sequence(block):
        return ordered(first_y, pick(block, y, 0), swap(pick(block, 1 - y, 0), "y"), 0)

    def own_tokens(rows):
        halves = rows.reshape(2, half_tokens, width)
        mine, theirs = pick(halves, y, 0), swap(pick(halves, 1 - y, 0), "y")
        return jnp.where(first_y, jnp.stack([mine, theirs]), jnp.stack([theirs, mine]))

    def core_columns(weight):
        parts = weight.reshape(weight.shape[0], 2, channels)
        return ordered(first_c, pick(parts, c, 1), swap(pick(parts, 1 - c, 1), "c"), 0)

    gains = jnp.stack([norm_gain, mlp_gain]).reshape(1, -1)
    gains = lax.all_to_all(jnp.tile(gains, (devices, 1)), EVERY, 0, 0, tiled=True)
    gains = jnp.swapaxes(gains.reshape(devices, 2, -1), 0, 1).reshape(2, width).astype(F32)
    ngain, mgain = gains[0], gains[1]

    vectors = jnp.concatenate(
        [conv_weight, conv_bias[None], rgate_bias[None], igate_bias[None], rate_param[None]]
    )
    vectors = jnp.pad(vectors.T, ((0, 0), (0, 120)))
    gate_shard = jnp.concatenate([w_rgate, w_igate, vectors], axis=1)
    gate_shard = lax.ppermute(gate_shard, EVERY, to_halves(devices))
    gates = whole_gather(gate_shard, "y", "x")
    branch_full = fine_gather(core_columns(w_branch), "y", "x")
    recur_in_full = fine_gather(core_columns(w_recur_in), "x", "y")
    out_shard = lax.ppermute(w_recur_out, EVERY, to_halves(devices))
    out_full = jnp.concatenate(
        [
            whole_gather(out_shard[:, : width // 2], "y", "x"),
            whole_gather(out_shard[:, width // 2 :], "x", "y"),
        ],
        axis=1,
    )

    units = w_gate.shape[1] // 2
    gate_up = jnp.stack([w_gate, w_up], 1).reshape(w_gate.shape[0], 2, 2, units)
    mine = pick(gate_up, y, 2).reshape(-1, 2 * units)
    theirs = swap(pick(gate_up, 1 - y, 2).reshape(-1, 2 * units), "y")
    gate_up_full = jnp.concatenate(z_gather(ordered(first_y, mine, theirs, 0)))
    down = w_down.reshape(2, units, -1)
    down_shard = ordered(first_y, pick(down, y, 0), swap(pick(down, 1 - y, 0), "y"), 1)
    down_full = jnp.concatenate(z_gather(down_shard), axis=1)

    vec = gates[:, 512:520].T.astype(F32)
    rate = vec[7]
    eight = -8.0 * jax.nn.softplus(rate)
    vec = jnp.concatenate([vec[:7], eight[None]])

    rows_in = own_sequence(block_input).astype(F32)
    normed_f, norm_pull = jax.vjp(rms_scale, rows_in, ngain)
    chips, places = fine_chips(), fine_places()
    normed = columns(low(normed_f), chips)
    normed = jnp.concatenate([normed, swap(normed, "c")])
    branch_pre = mm(normed, branch_full)
    recur_pre = mm(normed, recur_in_full).reshape(2, length, channels)
    branch_act, gelu_pull = jax.vjp(partial(jax.nn.gelu, approximate=True), branch_pre)
    halo = z_shift(recur_pre[:, length - 8 :], 1)
    conv, sig_r, sig_i, decay, state, prod = run_forward(recur_pre, halo, vec, gates)
    carry = z_carry(prod[:, -1], state[:, -1], 1)
    states = (state + prod * carry[:, None]).reshape(2 * length, channels)
    mixed_low = low(states * branch_act)
    recur_out = mm(mixed_low, out_full)
    middle = rows_in + recur_out[:length] + swap(recur_out[length:], "c")

    normed2_f, norm2_pull = jax.vjp(rms_scale, middle, mgain)
    tokens_all = group_gather(columns(low(normed2_f), z_places))
    pre = mm(tokens_all, gate_up_full)
    hidden_f, mlp_pull = jax.vjp(mlp_act, pre[:, :units], pre[:, units:])
    hidden = low(hidden_f)
    mlp_out = columns(group_scatter(mm(hidden, down_full)), z_back)
    block_output = own_tokens(low(middle + mlp_out))

    own_grad = own_sequence(cotangent)
    grad_all = group_gather(columns(own_grad, z_places))
    grad_hidden = mm_rows(grad_all, down_full)
    grad_pre = jnp.concatenate([low(g) for g in mlp_pull(grad_hidden)], axis=1)
    grad_normed2 = columns(group_scatter(mm_rows(grad_pre, gate_up_full)), z_back)
    block = width // z_count
    grad_gate_up = z_scatter(
        lambda j: outer_sum(tokens_all[:, j * block : (j + 1) * block], grad_pre)
    )
    grad_down = z_scatter(lambda j: outer_sum(hidden, grad_all[:, j * block : (j + 1) * block]))
    grad_gate_up = grad_gate_up.reshape(2, block // 2, 2 * units)
    kept, other = pick(grad_gate_up, y, 0), swap(low(pick(grad_gate_up, 1 - y, 0)), "y")
    kept = kept.reshape(-1, 2, 1, units)
    other = other.astype(F32).reshape(-1, 2, 1, units)
    both = ordered(first_y, kept, other, 2).reshape(-1, 2, 2 * units)
    grad_gate, grad_up = both[:, 0], both[:, 1]
    grad_down = grad_down.reshape(units, 2, -1)
    kept, other = pick(grad_down, y, 1), swap(low(pick(grad_down, 1 - y, 1)), "y")
    grad_down = ordered(first_y, kept, other.astype(F32), 0)

    grad_middle_norm, grad_mgain = norm2_pull(grad_normed2)
    grad_middle = own_grad.astype(F32) + grad_middle_norm
    grad_out_low = low(grad_middle)
    grad_out_low = jnp.concatenate([grad_out_low, swap(grad_out_low, "c")])
    grad_mixed = mm_rows(grad_out_low, out_full)
    grad_states = (grad_mixed * branch_act).reshape(2, length, channels)
    grad_branch_low = low(gelu_pull(grad_mixed * states)[0])
    local, ahead, sent = run_reverse(decay, grad_states)
    entering = z_carry(prod[:, -1], sent, -1)
    grad_conv, grad_rgate, grad_igate, small = run_backward(
        local, ahead, entering, state, prod, carry, conv, sig_r, sig_i, recur_pre, halo, vec, gates
    )
    rim = z_shift(grad_conv[:, :8], -1)
    grad_ext = jnp.concatenate([grad_conv, rim], axis=1)
    grad_recur_low = low(sum(vec[k] * grad_ext[:, k : k + length] for k in range(CONV)))
    grad_recur_low = grad_recur_low.reshape(2 * length, channels)
    grad_normed = mm_rows(grad_branch_low, branch_full) + mm_rows(grad_recur_low, recur_in_full)
    grad_normed = grad_normed[:length] + swap(grad_normed[length:], "c")
    grad_rows, grad_ngain = norm_pull(columns(grad_normed, places))
    input_grad = own_tokens(low(grad_middle + grad_rows))

    def own_rows(chunk):
        parts = chunk.reshape(2, -1, channels)
        return ordered(first_c, pick(parts, c, 0), swap(pick(parts, 1 - c, 0), "c"), 1)

    from_halves = [(target, source) for source, target in to_halves(devices)]
    grad_out_w = outer_sum(mixed_low, grad_out_low)
    grad_out_w = jnp.concatenate(
        [
            whole_scatter(grad_out_w[:, : width // 2], "y", "x"),
            whole_scatter(grad_out_w[:, width // 2 :], "x", "y"),
        ],
        axis=1,
    )
    grad_recur_out = lax.ppermute(low(grad_out_w), EVERY, from_halves).astype(F32)
    small = jnp.concatenate([small[:7], (small[7] * -8.0 * jax.nn.sigmoid(rate))[None]])
    small = jnp.pad(small.T, ((0, 0), (0, 120)))
    gate_grads = jnp.concatenate([grad_rgate, grad_igate, small], axis=1)
    gate_grads = lax.ppermute(whole_scatter(gate_grads, "y", "x"), EVERY, from_halves)
    small = gate_grads[:, 512:520].T
    grad_branch = own_rows(fine_scatter(outer_sum(normed, grad_branch_low), "y", "x"))
    grad_recur_in = own_rows(fine_scatter(outer_sum(normed, grad_recur_low), "x", "y"))
    gain_grads = jnp.stack([grad_ngain, grad_mgain]).reshape(2, devices, -1)
    gain_grads = jnp.swapaxes(gain_grads, 0, 1).reshape(devices, -1)
    gain_grads = lax.all_to_all(gain_grads, EVERY, 0, 0, tiled=True)
    gain_grads = jnp.sum(gain_grads, axis=0).reshape(2, -1)
    return (
        block_output,
        input_grad,
        grad_branch,
        grad_recur_in,
        grad_recur_out,
        gate_grads[:, :256],
        gate_grads[:, 256:512],
        small[:4],
        small[4],
        small[5],
        small[6],
        small[7],
        gain_grads[0],
        gain_grads[1],
        grad_gate,
        grad_up,
        grad_down,
    )


def solution(mesh):
    seq, mlp = mesh.shape["seq"], mesh.shape["mlp"]
    fine = Mesh(mesh.devices.reshape(seq // 2, 2, mlp // 2, 2), EVERY)
    over_seq, over_mlp = ("z", "y"), ("x", "c")
    rows, channel, vector = P(EVERY, None), P(None, EVERY), P(EVERY)
    tokens = P(over_mlp, over_seq, None)
    in_specs = (
        (tokens,) + (rows,) * 5 + (channel,) + (vector,) * 6
        + (P(over_seq, over_mlp), P(over_seq, over_mlp), P(over_mlp, over_seq), tokens)
    )
    out_specs = (
        (tokens, tokens) + (rows,) * 5 + (channel,) + (vector,) * 6
        + (P(over_seq, over_mlp), P(over_seq, over_mlp), P(over_mlp, over_seq))
    )
    return jax.shard_map(
        on_device, mesh=fine, in_specs=in_specs, out_specs=out_specs, check_vma=False
    )
```

```python
from functools import partial

import jax
import jax.numpy as jnp
from jax import lax
from jax.experimental import pallas as pl
from jax.experimental.pallas import tpu as pltpu
from jax.sharding import Mesh, PartitionSpec as P

HEADS = 10
CONV = 4
F32 = jnp.float32
BF16 = jnp.bfloat16
PAIR = ((0, 1), (1, 0))


def swap(value, axis):
    return lax.ppermute(value, axis, PAIR)


def low(value):
    return value.astype(BF16)


def ordered(first, mine, theirs, axis):
    return jnp.where(
        first, jnp.concatenate([mine, theirs], axis), jnp.concatenate([theirs, mine], axis)
    )


def pick(array, index, axis):
    return lax.dynamic_index_in_dim(array, index, axis, keepdims=False)


def z_direct():
    return lax.axis_size("z") == 4


def z_send(value, j):
    count = lax.axis_size("z")
    return lax.ppermute(value, "z", [(s, s ^ j) for s in range(count)])


def place(pieces, size):
    rows = pieces[0][1].shape[0]
    full = jnp.zeros((size * rows,) + pieces[0][1].shape[1:], pieces[0][1].dtype)
    for at, piece in pieces:
        full = lax.dynamic_update_slice_in_dim(full, piece, at * rows, 0)
    return full


def z_gather(shard):
    count = lax.axis_size("z")
    if not z_direct():
        return lax.all_gather(shard, "z", axis=0, tiled=True)
    z = lax.axis_index("z")
    pieces = [(z, shard)] + [(z ^ j, z_send(shard, j)) for j in range(1, count)]
    return place(pieces, count)


def z_scatter(part):
    count = lax.axis_size("z")
    if not z_direct():
        return lax.psum_scatter(low(part), "z", scatter_dimension=0, tiled=True).astype(F32)
    z, rows = lax.axis_index("z"), part.shape[0] // count
    total = lax.dynamic_slice_in_dim(part, z * rows, rows, 0)
    for j in range(1, count):
        block = lax.dynamic_slice_in_dim(part, (z ^ j) * rows, rows, 0)
        total = total + z_send(low(block), j).astype(F32)
    return total


def z_shift(value, steps):
    count = lax.axis_size("z")
    return lax.ppermute(
        value, "z", [(s, s + steps) for s in range(count) if 0 <= s + steps < count]
    )


def z_carry(decay, state, step):
    count = lax.axis_size("z")
    pair = jnp.stack([decay, state])
    if z_direct():
        near = [z_shift(pair, step * k) for k in range(1, count)]
        carry = near[-1][1]
        for got in near[-2::-1]:
            carry = got[1] + got[0] * carry
        return carry
    everything, here = lax.all_gather(pair, "z"), lax.axis_index("z")

    def hop(k, before):
        at = k if step == 1 else count - 1 - k
        reached = at < here if step == 1 else at > here
        return jnp.where(reached, everything[at, 1] + everything[at, 0] * before, before)

    return lax.fori_loop(0, count, hop, jnp.zeros_like(state))


def group_gather(own):
    half = own.shape[0] // 2
    over_x, over_y = swap(own, "x"), swap(own, "y")
    corner = jnp.concatenate([swap(over_x[:half], "y"), swap(over_y[half:], "x")])
    near = jnp.concatenate([over_x, over_y, corner])
    return jnp.concatenate([own, near, swap(own, "c"), swap(near, "c")])


def group_scatter(partial_sum):
    rows = partial_sum.shape[0] // 8
    mine = partial_sum[: 4 * rows] + swap(low(partial_sum[4 * rows :]), "c").astype(F32)
    own, to_x, to_y, corner = (mine[k * rows : (k + 1) * rows] for k in range(4))
    half = rows // 2
    via_x = swap(low(corner[:half]), "x").astype(F32)
    via_y = swap(low(corner[half:]), "y").astype(F32)
    to_y = jnp.concatenate([to_y[:half] + via_x, to_y[half:]])
    to_x = jnp.concatenate([to_x[:half], to_x[half:] + via_y])
    return own + swap(low(to_x), "x").astype(F32) + swap(low(to_y), "y").astype(F32)


def fine_order(values):
    count = lax.axis_size("z")
    blocks = values.reshape(values.shape[0], count, 2, 2, -1)
    return jnp.transpose(blocks, (0, 3, 2, 1, 4)).reshape(values.shape)


def fine_back(values):
    count = lax.axis_size("z")
    blocks = values.reshape(values.shape[0], 2, 2, count, -1)
    return jnp.transpose(blocks, (0, 3, 2, 1, 4)).reshape(values.shape)


def fine_gather(own, first, second):
    x, y = lax.axis_index("x"), lax.axis_index("y")
    far = swap(own, second)
    near = swap(own, first)
    both = swap(near, second)
    over_y, over_x = (near, far) if first == "y" else (far, near)
    return place(
        [
            (2 * x + y, own),
            (2 * x + (1 - y), over_y),
            (2 * (1 - x) + y, over_x),
            (2 * (1 - x) + (1 - y), both),
        ],
        4,
    )


def fine_near(part, first, second):
    x, y = lax.axis_index("x"), lax.axis_index("y")

    def block(on_first, on_second):
        over_x, over_y = (on_second, on_first) if second == "x" else (on_first, on_second)
        return part(2 * (x ^ over_x) + (y ^ over_y))

    corner = swap(low(block(1, 1)), second)
    far = swap(low(block(0, 1)), second)
    return block, corner, far, lambda got: swap(low(block(1, 0) + got.astype(F32)), first)


def fine_total(block, far, near):
    return block(0, 0) + far.astype(F32) + near.astype(F32)


def to_halves(count):
    return [(count // 2 * c + q, 2 * q + c) for q in range(count // 2) for c in range(2)]


EVERY = ("z", "y", "x", "c")
CHIPS = ("z", "y", "x")


def expm1_neg(value):
    series = 1.0
    for k in range(10, 1, -1):
        series = 1.0 + value / k * series
    return jnp.where(value > -1.0, -value * series, 1.0 - jnp.exp(value))


def forward_kernel(
    rec_ref, halo_ref, vec_ref, wr_ref, wi_ref, conv_ref, sr_ref, si_ref, a_ref, s_ref, p_ref, ext
):
    head, heads = pl.program_id(0), pl.num_programs(0)
    seqs, length, width = rec_ref.shape
    lanes = pl.ds(pl.multiple_of(head * width, width), width)
    vec = vec_ref[...]
    for s in range(seqs):
        ext[s, 0:8, :] = halo_ref[s]
        ext[s, 8 : 8 + length, :] = rec_ref[s]
        conv = vec[4:5] + sum(
            vec[k : k + 1] * ext[s, 8 - k : 8 - k + length, :] for k in range(CONV)
        )
        conv_low = low(conv)
        sig_r = jax.nn.sigmoid(
            jnp.dot(conv_low, wr_ref[...], preferred_element_type=F32) + vec[5:6]
        )
        sig_i = jax.nn.sigmoid(
            jnp.dot(conv_low, wi_ref[...], preferred_element_type=F32) + vec[6:7]
        )
        decay_log = vec[7:8] * sig_r
        conv_ref[s] = conv
        sr_ref[s] = sig_r
        si_ref[s] = sig_i
        a_ref[s, :, lanes] = jnp.exp(decay_log)
        s_ref[s, :, lanes] = sig_i * conv * jnp.sqrt(expm1_neg(2.0 * decay_log))

    @pl.when(head == heads - 1)
    def _():
        def step(t, carry):
            new = []
            for s in range(seqs):
                prod, state = carry[s]
                row = pl.ds(t, 1)
                decay = a_ref[s, row, :]
                prod = decay * prod
                state = decay * state + s_ref[s, row, :]
                p_ref[s, row, :] = prod
                s_ref[s, row, :] = state
                new.append((prod, state))
            return tuple(new)

        full = a_ref.shape[2]
        start = (jnp.ones((1, full), F32), jnp.zeros((1, full), F32))
        lax.fori_loop(0, length, step, (start,) * seqs)


def reverse_kernel(a_ref, g_ref, l_ref, q_ref, e_ref):
    seqs, length, full = a_ref.shape

    def step(k, carry):
        t = length - 1 - k
        new = []
        for s in range(seqs):
            prod, sent = carry[s]
            row = pl.ds(t, 1)
            q_ref[s, row, :] = prod
            delta = g_ref[s, row, :] + sent
            l_ref[s, row, :] = delta
            decay = a_ref[s, row, :]
            new.append((prod * decay, decay * delta))
        return tuple(new)

    start = (jnp.ones((1, full), F32), jnp.zeros((1, full), F32))
    last = lax.fori_loop(0, length, step, (start,) * seqs)
    for s in range(seqs):
        e_ref[pl.ds(s, 1), :] = last[s][1]


def backward_kernel(
    l_ref, q_ref, e_ref, s_ref, p_ref, carry_ref, conv_ref, sr_ref, si_ref, rec_ref, halo_ref,
    vec_ref, wr_ref, wi_ref, gconv_ref, gwr_ref, gwi_ref, small_ref, ext, before,
):
    seqs, length, width = rec_ref.shape
    vec = vec_ref[...]
    rows = [jnp.zeros((1, width), F32)] * 8
    contract_rows = (((0,), (0,)), ((), ()))
    contract_last = (((1,), (1,)), ((), ()))
    for s in range(seqs):
        ext[s, 0:8, :] = halo_ref[s]
        ext[s, 8 : 8 + length, :] = rec_ref[s]
        carry = carry_ref[s : s + 1, :]
        before[s, 0:8, :] = jnp.broadcast_to(carry, (8, width))
        before[s, 8 : 8 + length, :] = s_ref[s] + p_ref[s] * carry
        prev = before[s, 7 : 7 + length, :]
        delta = l_ref[s] + q_ref[s] * e_ref[s : s + 1, :]
        conv, sig_r, sig_i = conv_ref[s], sr_ref[s], si_ref[s]
        decay_log = vec[7:8] * sig_r
        decay = jnp.exp(decay_log)
        scale = jnp.sqrt(expm1_neg(2.0 * decay_log))
        through = delta * sig_i
        grad_log = delta * prev * decay - through * conv * decay * decay / scale
        slope_r = grad_log * sig_r
        rows[7] = rows[7] + jnp.sum(slope_r, axis=0, keepdims=True)
        grad_r = low(slope_r * vec[7:8] * (1.0 - sig_r))
        grad_i = low(through * conv * scale * (1.0 - sig_i))
        conv_low = low(conv)
        gwr = lax.dot_general(conv_low, grad_r, contract_rows, preferred_element_type=F32)
        gwi = lax.dot_general(conv_low, grad_i, contract_rows, preferred_element_type=F32)
        if s == 0:
            gwr_ref[...], gwi_ref[...] = gwr, gwi
        else:
            gwr_ref[...] += gwr
            gwi_ref[...] += gwi
        rows[5] = rows[5] + jnp.sum(grad_r.astype(F32), axis=0, keepdims=True)
        rows[6] = rows[6] + jnp.sum(grad_i.astype(F32), axis=0, keepdims=True)
        grad_conv = (
            through * scale
            + lax.dot_general(grad_r, wr_ref[...], contract_last, preferred_element_type=F32)
            + lax.dot_general(grad_i, wi_ref[...], contract_last, preferred_element_type=F32)
        )
        gconv_ref[s] = grad_conv
        rows[4] = rows[4] + jnp.sum(grad_conv, axis=0, keepdims=True)
        for k in range(CONV):
            tap = grad_conv * ext[s, 8 - k : 8 - k + length, :]
            rows[k] = rows[k] + jnp.sum(tap, axis=0, keepdims=True)
    for k in range(8):
        small_ref[k : k + 1, :] = rows[k]


def cost(flops, values):
    return pl.CostEstimate(flops=flops, bytes_accessed=values, transcendentals=0)


def run_forward(rec, halo, vec, gates):
    seqs, length, full = rec.shape
    heads = HEADS // 2
    width = full // heads
    column = (gates.shape[1] - 640) // width
    block = pl.BlockSpec((seqs, length, width), lambda h: (0, 0, h))
    whole = pl.BlockSpec((seqs, length, full), lambda h: (0, 0, 0))
    array = jax.ShapeDtypeStruct(rec.shape, F32)
    return pl.pallas_call(
        forward_kernel,
        grid=(heads,),
        in_specs=[
            block,
            pl.BlockSpec((seqs, 8, width), lambda h: (0, 0, h)),
            pl.BlockSpec((8, width), lambda h: (0, h)),
            pl.BlockSpec((width, width), lambda h: (h, column)),
            pl.BlockSpec((width, width), lambda h: (h, column + 1)),
        ],
        out_specs=[block, block, block, whole, whole, whole],
        out_shape=[array] * 6,
        scratch_shapes=[pltpu.VMEM((seqs, length + 8, width), F32)],
        cost_estimate=cost(seqs * length * full * width * 4, rec.size * 28),
        name="recur_forward",
    )(rec, halo, vec, gates, gates)


def run_reverse(decay, grad_states):
    seqs, length, full = decay.shape
    array = jax.ShapeDtypeStruct(decay.shape, F32)
    return pl.pallas_call(
        reverse_kernel,
        out_shape=[array, array, jax.ShapeDtypeStruct((seqs, full), F32)],
        cost_estimate=cost(decay.size * 4, decay.size * 16),
        name="recur_reverse",
    )(decay, grad_states)


def run_backward(local, ahead, entering, state, prod, carry, conv, sig_r, sig_i, rec, halo, vec, gates):
    seqs, length, full = rec.shape
    heads = HEADS // 2
    width = full // heads
    column = (gates.shape[1] - 640) // width
    block = pl.BlockSpec((seqs, length, width), lambda h: (0, 0, h))
    row = pl.BlockSpec((seqs, width), lambda h: (0, h))
    weight = pl.BlockSpec((width, width), lambda h: (h, 0))
    return pl.pallas_call(
        backward_kernel,
        grid=(heads,),
        in_specs=[
            block,
            block,
            row,
            block,
            block,
            row,
            block,
            block,
            block,
            block,
            pl.BlockSpec((seqs, 8, width), lambda h: (0, 0, h)),
            pl.BlockSpec((8, width), lambda h: (0, h)),
            pl.BlockSpec((width, width), lambda h: (h, column)),
            pl.BlockSpec((width, width), lambda h: (h, column + 1)),
        ],
        out_specs=[block, weight, weight, pl.BlockSpec((8, width), lambda h: (0, h))],
        out_shape=[
            jax.ShapeDtypeStruct(rec.shape, F32),
            jax.ShapeDtypeStruct((full, width), F32),
            jax.ShapeDtypeStruct((full, width), F32),
            jax.ShapeDtypeStruct((8, full), F32),
        ],
        scratch_shapes=[pltpu.VMEM((seqs, length + 8, width), F32)] * 2,
        cost_estimate=cost(seqs * length * full * width * 8, rec.size * 40),
        name="recur_backward",
    )(local, ahead, entering, state, prod, carry, conv, sig_r, sig_i, rec, halo, vec, gates, gates)


def rms_scale(values, gain):
    return values * lax.rsqrt(jnp.mean(values * values, axis=-1, keepdims=True) + 1e-06) * gain


def mlp_act(gate_pre, up_pre):
    return jax.nn.gelu(gate_pre, approximate=True) * up_pre


def mm(left, right):
    return jnp.dot(left, right, preferred_element_type=F32)


def mm_rows(left, weight):
    return lax.dot_general(left, weight, (((1,), (1,)), ((), ())), preferred_element_type=F32)


def outer_sum(left, right):
    return lax.dot_general(left, right, (((0,), (0,)), ((), ())), preferred_element_type=F32)


def on_device(
    block_input,
    w_branch,
    w_recur_in,
    w_recur_out,
    w_rgate,
    w_igate,
    conv_weight,
    conv_bias,
    rgate_bias,
    igate_bias,
    rate_param,
    norm_gain,
    mlp_gain,
    w_gate,
    w_up,
    w_down,
    cotangent,
):
    z, y, c = (lax.axis_index(axis) for axis in ("z", "y", "c"))
    z_count = lax.axis_size("z")
    devices = z_count * 8
    first_y, first_c = y == 0, c == 0
    half_tokens, width = block_input.shape[1:]
    length = 2 * half_tokens
    channels = w_branch.shape[1] // 2

    def own_sequence(block):
        return ordered(first_y, pick(block, y, 0), swap(pick(block, 1 - y, 0), "y"), 0)

    def own_tokens(rows):
        halves = rows.reshape(2, half_tokens, width)
        mine, theirs = pick(halves, y, 0), swap(pick(halves, 1 - y, 0), "y")
        return jnp.where(first_y, jnp.stack([mine, theirs]), jnp.stack([theirs, mine]))

    def core_columns(weight):
        parts = weight.reshape(weight.shape[0], 2, channels)
        return ordered(first_c, pick(parts, c, 1), swap(pick(parts, 1 - c, 1), "c"), 0)

    branch_shard, recur_in_shard = core_columns(w_branch), core_columns(w_recur_in)
    (
        branch_shard, recur_in_shard, w_recur_out, w_rgate, w_gate, w_up, w_down, norm_gain
    ) = lax.optimization_barrier(
        (branch_shard, recur_in_shard, w_recur_out, w_rgate, w_gate, w_up, w_down, norm_gain)
    )

    gains = jnp.stack([norm_gain, mlp_gain]).reshape(1, -1)
    gains = lax.all_to_all(jnp.tile(gains, (devices, 1)), EVERY, 0, 0, tiled=True)
    gains = jnp.swapaxes(gains.reshape(devices, 2, -1), 0, 1).reshape(2, width).astype(F32)
    ngain, mgain = gains[0], gains[1]

    vectors = jnp.concatenate(
        [conv_weight, conv_bias[None], rgate_bias[None], igate_bias[None], rate_param[None]]
    )
    vectors = jnp.pad(vectors.T, ((0, 0), (0, 120)))
    out_gates = jnp.concatenate([w_recur_out, w_rgate, w_igate, vectors], axis=1)
    out_gates = lax.ppermute(out_gates, EVERY, to_halves(devices))
    out_gates = lax.all_gather(out_gates, CHIPS, axis=0, tiled=True)
    out_full = out_gates[:, :width]
    branch_full = fine_gather(z_gather(branch_shard), "y", "x")
    recur_in_full = fine_gather(z_gather(recur_in_shard), "x", "y")

    units = w_gate.shape[1] // 2
    gate_up = jnp.stack([w_gate, w_up], 1).reshape(w_gate.shape[0], 2, 2, units)
    mine = pick(gate_up, y, 2).reshape(-1, 2 * units)
    theirs = swap(pick(gate_up, 1 - y, 2).reshape(-1, 2 * units), "y")
    gate_up_shard = ordered(first_y, mine, theirs, 0)
    gate_up_full = lax.all_gather(gate_up_shard, "z", axis=0, tiled=True)
    down = w_down.reshape(2, units, -1)
    down_shard = ordered(first_y, pick(down, y, 0), swap(pick(down, 1 - y, 0), "y"), 1)
    down_full = lax.all_gather(down_shard, "z", axis=0)
    down_full = jnp.swapaxes(down_full, 0, 1).reshape(units, width)

    vec = out_gates[:, width + 512 : width + 520].T.astype(F32)
    rate = vec[7]
    eight = -8.0 * jax.nn.softplus(rate)
    vec = jnp.concatenate([vec[:7], eight[None]])

    rows_in = own_sequence(block_input).astype(F32)
    normed_f, norm_pull = jax.vjp(rms_scale, rows_in, ngain)
    normed = fine_order(low(normed_f))
    normed = jnp.concatenate([normed, swap(normed, "c")])
    branch_pre = mm(normed, branch_full)
    recur_pre = mm(normed, recur_in_full).reshape(2, length, channels)
    branch_act, gelu_pull = jax.vjp(partial(jax.nn.gelu, approximate=True), branch_pre)
    halo = z_shift(recur_pre[:, length - 8 :], 1)
    conv, sig_r, sig_i, decay, state, prod = run_forward(recur_pre, halo, vec, out_gates)
    carry = z_carry(prod[:, -1], state[:, -1], 1)
    states = (state + prod * carry[:, None]).reshape(2 * length, channels)
    mixed_low = low(states * branch_act)
    recur_out = mm(mixed_low, out_full)
    middle = rows_in + recur_out[:length] + swap(recur_out[length:], "c")

    normed2_f, norm2_pull = jax.vjp(rms_scale, middle, mgain)
    tokens_all = group_gather(low(normed2_f))
    pre = mm(tokens_all, gate_up_full)
    hidden_f, mlp_pull = jax.vjp(mlp_act, pre[:, :units], pre[:, units:])
    hidden = low(hidden_f)
    mlp_out = group_scatter(mm(hidden, down_full))
    block_output = own_tokens(low(middle + mlp_out))

    own_grad = own_sequence(cotangent)
    grad_all = group_gather(own_grad)
    grad_hidden = mm_rows(grad_all, down_full)
    grad_pre = jnp.concatenate([low(g) for g in mlp_pull(grad_hidden)], axis=1)
    grad_normed2 = group_scatter(mm_rows(grad_pre, gate_up_full))
    block = width // z_count
    grad_gate_up = lax.psum_scatter(
        low(outer_sum(tokens_all, grad_pre)), "z", scatter_dimension=0, tiled=True
    ).astype(F32)
    grad_down = lax.psum_scatter(
        low(outer_sum(grad_all, hidden)), "z", scatter_dimension=0, tiled=True
    ).astype(F32)
    grad_gate_up = grad_gate_up.reshape(2, block // 2, 2 * units)
    gate_up_kept = pick(grad_gate_up, y, 0).reshape(-1, 2, 1, units)
    gate_up_other = swap(low(pick(grad_gate_up, 1 - y, 0)), "y")
    grad_down = grad_down.reshape(2, -1, units)
    down_kept, down_other = pick(grad_down, y, 0), swap(low(pick(grad_down, 1 - y, 0)), "y")

    grad_middle_norm, grad_mgain = norm2_pull(grad_normed2)
    grad_middle = own_grad.astype(F32) + grad_middle_norm
    grad_out_low = low(grad_middle)
    grad_out_low = jnp.concatenate([grad_out_low, swap(grad_out_low, "c")])
    grad_mixed = mm_rows(grad_out_low, out_full)
    grad_states = (grad_mixed * branch_act).reshape(2, length, channels)
    grad_branch_low = low(gelu_pull(grad_mixed * states)[0])
    local, ahead, sent = run_reverse(decay, grad_states)
    entering = z_carry(prod[:, -1], sent, -1)
    grad_conv, grad_rgate, grad_igate, small = run_backward(
        local, ahead, entering, state, prod, carry, conv, sig_r, sig_i, recur_pre, halo, vec, out_gates
    )

    def quarter(grad):
        def part(at):
            rows = lax.dynamic_slice_in_dim(normed, at * (width // 4), width // 4, 1)
            return outer_sum(rows, grad)

        return part

    block, corner, far, onward = fine_near(quarter(grad_branch_low), "y", "x")
    grad_conv, corner = lax.optimization_barrier((grad_conv, corner))
    near = onward(corner)
    rim = z_shift(grad_conv[:, :8], -1)
    grad_ext = jnp.concatenate([grad_conv, rim], axis=1)
    grad_recur_low = low(sum(vec[k] * grad_ext[:, k : k + length] for k in range(CONV)))
    grad_recur_low = grad_recur_low.reshape(2 * length, channels)
    grad_recur_low, far, near = lax.optimization_barrier((grad_recur_low, far, near))
    branch_near = fine_total(block, far, near)
    grad_normed = mm_rows(grad_branch_low, branch_full) + mm_rows(grad_recur_low, recur_in_full)
    grad_normed = grad_normed[:length] + swap(grad_normed[length:], "c")
    grad_rows, grad_ngain = norm_pull(fine_back(grad_normed))
    input_rows = low(grad_middle + grad_rows)

    def own_rows(chunk):
        parts = chunk.reshape(2, -1, channels)
        return ordered(first_c, pick(parts, c, 0), swap(pick(parts, 1 - c, 0), "c"), 1)

    from_halves = [(target, source) for source, target in to_halves(devices)]
    small = jnp.concatenate([small[:7], (small[7] * -8.0 * jax.nn.sigmoid(rate))[None]])
    small = jnp.pad(small.T, ((0, 0), (0, 120)))
    out_grads = [low(g) for g in (outer_sum(mixed_low, grad_out_low), grad_rgate, grad_igate, small)]
    out_grads = jnp.concatenate(out_grads, axis=1)
    out_grads = lax.psum_scatter(out_grads, CHIPS, scatter_dimension=0, tiled=True)
    out_grads = lax.ppermute(out_grads, EVERY, from_halves).astype(F32)
    grad_recur_out, gate_grads = out_grads[:, :width], out_grads[:, width:]
    small = gate_grads[:, 512:520].T
    grad_branch = own_rows(z_scatter(branch_near))
    block, corner, far, onward = fine_near(quarter(grad_recur_low), "x", "y")
    recur_in_near = fine_total(block, far, onward(corner))
    (
        recur_in_near, gate_up_other, down_other, grad_ngain, grad_mgain, input_rows
    ) = lax.optimization_barrier(
        (recur_in_near, gate_up_other, down_other, grad_ngain, grad_mgain, input_rows)
    )
    grad_recur_in = own_rows(z_scatter(recur_in_near))
    input_grad = own_tokens(input_rows)
    gate_up_other = gate_up_other.astype(F32).reshape(-1, 2, 1, units)
    both = ordered(first_y, gate_up_kept, gate_up_other, 2).reshape(-1, 2, 2 * units)
    grad_gate, grad_up = both[:, 0], both[:, 1]
    grad_down = ordered(first_y, down_kept, down_other.astype(F32), 1).T
    gain_grads = jnp.stack([grad_ngain, grad_mgain])
    for axis in ("c", "x", "y"):
        gain_grads = gain_grads + swap(gain_grads, axis)
    if z_direct():
        gain_grads = gain_grads + sum(z_send(gain_grads, j) for j in range(1, z_count))
    else:
        gain_grads = lax.psum(gain_grads, "z")
    gain_grads = pick(gain_grads.reshape(2, devices, -1), lax.axis_index(EVERY), 1)
    return (
        block_output,
        input_grad,
        grad_branch,
        grad_recur_in,
        grad_recur_out,
        gate_grads[:, :256],
        gate_grads[:, 256:512],
        small[:4],
        small[4],
        small[5],
        small[6],
        small[7],
        gain_grads[0],
        gain_grads[1],
        grad_gate,
        grad_up,
        grad_down,
    )


def solution(mesh):
    seq, mlp = mesh.shape["seq"], mesh.shape["mlp"]
    fine = Mesh(mesh.devices.reshape(seq // 2, 2, mlp // 2, 2), EVERY)
    over_seq, over_mlp = ("z", "y"), ("x", "c")
    rows, channel, vector = P(EVERY, None), P(None, EVERY), P(EVERY)
    tokens = P(over_mlp, over_seq, None)
    in_specs = (
        (tokens,) + (rows,) * 5 + (channel,) + (vector,) * 6
        + (P(over_seq, over_mlp), P(over_seq, over_mlp), P(over_mlp, over_seq), tokens)
    )
    out_specs = (
        (tokens, tokens) + (rows,) * 5 + (channel,) + (vector,) * 6
        + (P(over_seq, over_mlp), P(over_seq, over_mlp), P(over_mlp, over_seq))
    )
    return jax.shard_map(
        on_device, mesh=fine, in_specs=in_specs, out_specs=out_specs, check_vma=False
    )
```

```python
from functools import partial

import jax
import jax.numpy as jnp
from jax import lax
from jax.experimental import pallas as pl
from jax.experimental.pallas import tpu as pltpu
from jax.sharding import Mesh, PartitionSpec as P

HEADS = 10
CONV = 4
F32 = jnp.float32
BF16 = jnp.bfloat16
PAIR = ((0, 1), (1, 0))


def swap(value, axis):
    return lax.ppermute(value, axis, PAIR)


def low(value):
    return value.astype(BF16)


def ordered(first, mine, theirs, axis):
    return jnp.where(
        first, jnp.concatenate([mine, theirs], axis), jnp.concatenate([theirs, mine], axis)
    )


def pick(array, index, axis):
    return lax.dynamic_index_in_dim(array, index, axis, keepdims=False)


def z_direct():
    return lax.axis_size("z") == 4


def z_send(value, j):
    count = lax.axis_size("z")
    return lax.ppermute(value, "z", [(s, s ^ j) for s in range(count)])


def place(pieces, size):
    rows = pieces[0][1].shape[0]
    full = jnp.zeros((size * rows,) + pieces[0][1].shape[1:], pieces[0][1].dtype)
    for at, piece in pieces:
        full = lax.dynamic_update_slice_in_dim(full, piece, at * rows, 0)
    return full


def z_gather(shard):
    count = lax.axis_size("z")
    if not z_direct():
        return lax.all_gather(shard, "z", axis=0, tiled=True)
    z = lax.axis_index("z")
    pieces = [(z, shard)] + [(z ^ j, z_send(shard, j)) for j in range(1, count)]
    return place(pieces, count)


def z_scatter(part):
    count = lax.axis_size("z")
    if not z_direct():
        return lax.psum_scatter(low(part), "z", scatter_dimension=0, tiled=True).astype(F32)
    z, rows = lax.axis_index("z"), part.shape[0] // count
    total = lax.dynamic_slice_in_dim(part, z * rows, rows, 0)
    for j in range(1, count):
        block = lax.dynamic_slice_in_dim(part, (z ^ j) * rows, rows, 0)
        total = total + z_send(low(block), j).astype(F32)
    return total


def z_shift(value, steps):
    count = lax.axis_size("z")
    return lax.ppermute(
        value, "z", [(s, s + steps) for s in range(count) if 0 <= s + steps < count]
    )


def z_carry(decay, state, step):
    count = lax.axis_size("z")
    pair = jnp.stack([decay, state])
    if z_direct():
        near = [z_shift(pair, step * k) for k in range(1, count)]
        carry = near[-1][1]
        for got in near[-2::-1]:
            carry = got[1] + got[0] * carry
        return carry
    everything, here = lax.all_gather(pair, "z"), lax.axis_index("z")

    def hop(k, before):
        at = k if step == 1 else count - 1 - k
        reached = at < here if step == 1 else at > here
        return jnp.where(reached, everything[at, 1] + everything[at, 0] * before, before)

    return lax.fori_loop(0, count, hop, jnp.zeros_like(state))


def group_gather(own):
    half = own.shape[0] // 2
    over_x, over_y = swap(own, "x"), swap(own, "y")
    corner = jnp.concatenate([swap(over_x[:half], "y"), swap(over_y[half:], "x")])
    near = jnp.concatenate([over_x, over_y, corner])
    return jnp.concatenate([own, near, swap(own, "c"), swap(near, "c")])


def group_scatter(partial_sum):
    rows = partial_sum.shape[0] // 8
    mine = partial_sum[: 4 * rows] + swap(low(partial_sum[4 * rows :]), "c").astype(F32)
    own, to_x, to_y, corner = (mine[k * rows : (k + 1) * rows] for k in range(4))
    half = rows // 2
    via_x = swap(low(corner[:half]), "x").astype(F32)
    via_y = swap(low(corner[half:]), "y").astype(F32)
    to_y = jnp.concatenate([to_y[:half] + via_x, to_y[half:]])
    to_x = jnp.concatenate([to_x[:half], to_x[half:] + via_y])
    return own + swap(low(to_x), "x").astype(F32) + swap(low(to_y), "y").astype(F32)


def fine_order(values):
    count = lax.axis_size("z")
    blocks = values.reshape(values.shape[0], count, 2, 2, -1)
    return jnp.transpose(blocks, (0, 3, 2, 1, 4)).reshape(values.shape)


def fine_back(values):
    count = lax.axis_size("z")
    blocks = values.reshape(values.shape[0], 2, 2, count, -1)
    return jnp.transpose(blocks, (0, 3, 2, 1, 4)).reshape(values.shape)


def fine_gather(own, first, second):
    x, y = lax.axis_index("x"), lax.axis_index("y")
    far = swap(own, second)
    near = swap(own, first)
    both = swap(near, second)
    over_y, over_x = (near, far) if first == "y" else (far, near)
    return place(
        [
            (2 * x + y, own),
            (2 * x + (1 - y), over_y),
            (2 * (1 - x) + y, over_x),
            (2 * (1 - x) + (1 - y), both),
        ],
        4,
    )


def fine_near(part, first, second):
    x, y = lax.axis_index("x"), lax.axis_index("y")

    def block(on_first, on_second):
        over_x, over_y = (on_second, on_first) if second == "x" else (on_first, on_second)
        return part(2 * (x ^ over_x) + (y ^ over_y))

    corner = swap(low(block(1, 1)), second)
    far = swap(low(block(0, 1)), second)
    return block, corner, far, lambda got: swap(low(block(1, 0) + got.astype(F32)), first)


def fine_total(block, far, near):
    return block(0, 0) + far.astype(F32) + near.astype(F32)


def to_halves(count):
    return [(count // 2 * c + q, 2 * q + c) for q in range(count // 2) for c in range(2)]


EVERY = ("z", "y", "x", "c")
CHIPS = ("z", "y", "x")


def expm1_neg(value):
    series = 1.0
    for k in range(10, 1, -1):
        series = 1.0 + value / k * series
    return jnp.where(value > -1.0, -value * series, 1.0 - jnp.exp(value))


def forward_kernel(
    rec_ref, halo_ref, vec_ref, wr_ref, wi_ref, conv_ref, sr_ref, si_ref, a_ref, s_ref, p_ref, ext
):
    head, heads = pl.program_id(0), pl.num_programs(0)
    seqs, length, width = rec_ref.shape
    lanes = pl.ds(pl.multiple_of(head * width, width), width)
    vec = vec_ref[...]
    for s in range(seqs):
        ext[s, 0:8, :] = halo_ref[s]
        ext[s, 8 : 8 + length, :] = rec_ref[s]
        conv = vec[4:5] + sum(
            vec[k : k + 1] * ext[s, 8 - k : 8 - k + length, :] for k in range(CONV)
        )
        conv_low = low(conv)
        sig_r = jax.nn.sigmoid(
            jnp.dot(conv_low, wr_ref[...], preferred_element_type=F32) + vec[5:6]
        )
        sig_i = jax.nn.sigmoid(
            jnp.dot(conv_low, wi_ref[...], preferred_element_type=F32) + vec[6:7]
        )
        decay_log = vec[7:8] * sig_r
        conv_ref[s] = conv
        sr_ref[s] = sig_r
        si_ref[s] = sig_i
        a_ref[s, :, lanes] = jnp.exp(decay_log)
        s_ref[s, :, lanes] = sig_i * conv * jnp.sqrt(expm1_neg(2.0 * decay_log))

    @pl.when(head == heads - 1)
    def _():
        def step(t, carry):
            new = []
            for s in range(seqs):
                prod, state = carry[s]
                row = pl.ds(t, 1)
                decay = a_ref[s, row, :]
                prod = decay * prod
                state = decay * state + s_ref[s, row, :]
                p_ref[s, row, :] = prod
                s_ref[s, row, :] = state
                new.append((prod, state))
            return tuple(new)

        full = a_ref.shape[2]
        start = (jnp.ones((1, full), F32), jnp.zeros((1, full), F32))
        lax.fori_loop(0, length, step, (start,) * seqs)


def reverse_kernel(a_ref, g_ref, l_ref, q_ref, e_ref):
    seqs, length, full = a_ref.shape

    def step(k, carry):
        t = length - 1 - k
        new = []
        for s in range(seqs):
            prod, sent = carry[s]
            row = pl.ds(t, 1)
            q_ref[s, row, :] = prod
            delta = g_ref[s, row, :] + sent
            l_ref[s, row, :] = delta
            decay = a_ref[s, row, :]
            new.append((prod * decay, decay * delta))
        return tuple(new)

    start = (jnp.ones((1, full), F32), jnp.zeros((1, full), F32))
    last = lax.fori_loop(0, length, step, (start,) * seqs)
    for s in range(seqs):
        e_ref[pl.ds(s, 1), :] = last[s][1]


def backward_kernel(
    l_ref, q_ref, e_ref, s_ref, p_ref, carry_ref, conv_ref, sr_ref, si_ref, rec_ref, halo_ref,
    vec_ref, wr_ref, wi_ref, gconv_ref, gwr_ref, gwi_ref, small_ref, ext, before,
):
    seqs, length, width = rec_ref.shape
    vec = vec_ref[...]
    rows = [jnp.zeros((1, width), F32)] * 8
    contract_rows = (((0,), (0,)), ((), ()))
    contract_last = (((1,), (1,)), ((), ()))
    for s in range(seqs):
        ext[s, 0:8, :] = halo_ref[s]
        ext[s, 8 : 8 + length, :] = rec_ref[s]
        carry = carry_ref[s : s + 1, :]
        before[s, 0:8, :] = jnp.broadcast_to(carry, (8, width))
        before[s, 8 : 8 + length, :] = s_ref[s] + p_ref[s] * carry
        prev = before[s, 7 : 7 + length, :]
        delta = l_ref[s] + q_ref[s] * e_ref[s : s + 1, :]
        conv, sig_r, sig_i = conv_ref[s], sr_ref[s], si_ref[s]
        decay_log = vec[7:8] * sig_r
        decay = jnp.exp(decay_log)
        scale = jnp.sqrt(expm1_neg(2.0 * decay_log))
        through = delta * sig_i
        grad_log = delta * prev * decay - through * conv * decay * decay / scale
        slope_r = grad_log * sig_r
        rows[7] = rows[7] + jnp.sum(slope_r, axis=0, keepdims=True)
        grad_r = low(slope_r * vec[7:8] * (1.0 - sig_r))
        grad_i = low(through * conv * scale * (1.0 - sig_i))
        conv_low = low(conv)
        gwr = lax.dot_general(conv_low, grad_r, contract_rows, preferred_element_type=F32)
        gwi = lax.dot_general(conv_low, grad_i, contract_rows, preferred_element_type=F32)
        if s == 0:
            gwr_ref[...], gwi_ref[...] = gwr, gwi
        else:
            gwr_ref[...] += gwr
            gwi_ref[...] += gwi
        rows[5] = rows[5] + jnp.sum(grad_r.astype(F32), axis=0, keepdims=True)
        rows[6] = rows[6] + jnp.sum(grad_i.astype(F32), axis=0, keepdims=True)
        grad_conv = (
            through * scale
            + lax.dot_general(grad_r, wr_ref[...], contract_last, preferred_element_type=F32)
            + lax.dot_general(grad_i, wi_ref[...], contract_last, preferred_element_type=F32)
        )
        gconv_ref[s] = grad_conv
        rows[4] = rows[4] + jnp.sum(grad_conv, axis=0, keepdims=True)
        for k in range(CONV):
            tap = grad_conv * ext[s, 8 - k : 8 - k + length, :]
            rows[k] = rows[k] + jnp.sum(tap, axis=0, keepdims=True)
    for k in range(8):
        small_ref[k : k + 1, :] = rows[k]


def cost(flops, values):
    return pl.CostEstimate(flops=flops, bytes_accessed=values, transcendentals=0)


def run_forward(rec, halo, vec, gates):
    seqs, length, full = rec.shape
    heads = HEADS // 2
    width = full // heads
    column = (gates.shape[1] - 640) // width
    block = pl.BlockSpec((seqs, length, width), lambda h: (0, 0, h))
    whole = pl.BlockSpec((seqs, length, full), lambda h: (0, 0, 0))
    array = jax.ShapeDtypeStruct(rec.shape, F32)
    return pl.pallas_call(
        forward_kernel,
        grid=(heads,),
        in_specs=[
            block,
            pl.BlockSpec((seqs, 8, width), lambda h: (0, 0, h)),
            pl.BlockSpec((8, width), lambda h: (0, h)),
            pl.BlockSpec((width, width), lambda h: (h, column)),
            pl.BlockSpec((width, width), lambda h: (h, column + 1)),
        ],
        out_specs=[block, block, block, whole, whole, whole],
        out_shape=[array] * 6,
        scratch_shapes=[pltpu.VMEM((seqs, length + 8, width), F32)],
        cost_estimate=cost(seqs * length * full * width * 4, rec.size * 28),
        name="recur_forward",
    )(rec, halo, vec, gates, gates)


def run_reverse(decay, grad_states):
    seqs, length, full = decay.shape
    array = jax.ShapeDtypeStruct(decay.shape, F32)
    return pl.pallas_call(
        reverse_kernel,
        out_shape=[array, array, jax.ShapeDtypeStruct((seqs, full), F32)],
        cost_estimate=cost(decay.size * 4, decay.size * 16),
        name="recur_reverse",
    )(decay, grad_states)


def run_backward(local, ahead, entering, state, prod, carry, conv, sig_r, sig_i, rec, halo, vec, gates):
    seqs, length, full = rec.shape
    heads = HEADS // 2
    width = full // heads
    column = (gates.shape[1] - 640) // width
    block = pl.BlockSpec((seqs, length, width), lambda h: (0, 0, h))
    row = pl.BlockSpec((seqs, width), lambda h: (0, h))
    weight = pl.BlockSpec((width, width), lambda h: (h, 0))
    return pl.pallas_call(
        backward_kernel,
        grid=(heads,),
        in_specs=[
            block,
            block,
            row,
            block,
            block,
            row,
            block,
            block,
            block,
            block,
            pl.BlockSpec((seqs, 8, width), lambda h: (0, 0, h)),
            pl.BlockSpec((8, width), lambda h: (0, h)),
            pl.BlockSpec((width, width), lambda h: (h, column)),
            pl.BlockSpec((width, width), lambda h: (h, column + 1)),
        ],
        out_specs=[block, weight, weight, pl.BlockSpec((8, width), lambda h: (0, h))],
        out_shape=[
            jax.ShapeDtypeStruct(rec.shape, F32),
            jax.ShapeDtypeStruct((full, width), F32),
            jax.ShapeDtypeStruct((full, width), F32),
            jax.ShapeDtypeStruct((8, full), F32),
        ],
        scratch_shapes=[pltpu.VMEM((seqs, length + 8, width), F32)] * 2,
        cost_estimate=cost(seqs * length * full * width * 8, rec.size * 40),
        name="recur_backward",
    )(local, ahead, entering, state, prod, carry, conv, sig_r, sig_i, rec, halo, vec, gates, gates)


def rms_scale(values, gain):
    return values * lax.rsqrt(jnp.mean(values * values, axis=-1, keepdims=True) + 1e-06) * gain


def mlp_act(gate_pre, up_pre):
    return jax.nn.gelu(gate_pre, approximate=True) * up_pre


def mm(left, right):
    return jnp.dot(left, right, preferred_element_type=F32)


def mm_rows(left, weight):
    return lax.dot_general(left, weight, (((1,), (1,)), ((), ())), preferred_element_type=F32)


def outer_sum(left, right):
    return lax.dot_general(left, right, (((0,), (0,)), ((), ())), preferred_element_type=F32)


def on_device(
    block_input,
    w_branch,
    w_recur_in,
    w_recur_out,
    w_rgate,
    w_igate,
    conv_weight,
    conv_bias,
    rgate_bias,
    igate_bias,
    rate_param,
    norm_gain,
    mlp_gain,
    w_gate,
    w_up,
    w_down,
    cotangent,
):
    z, y, c = (lax.axis_index(axis) for axis in ("z", "y", "c"))
    z_count = lax.axis_size("z")
    devices = z_count * 8
    first_y, first_c = y == 0, c == 0
    half_tokens, width = block_input.shape[1:]
    length = 2 * half_tokens
    channels = w_branch.shape[1] // 2

    def own_sequence(block):
        return ordered(first_y, pick(block, y, 0), swap(pick(block, 1 - y, 0), "y"), 0)

    def own_tokens(rows):
        halves = rows.reshape(2, half_tokens, width)
        mine, theirs = pick(halves, y, 0), swap(pick(halves, 1 - y, 0), "y")
        return jnp.where(first_y, jnp.stack([mine, theirs]), jnp.stack([theirs, mine]))

    def core_columns(weight):
        parts = weight.reshape(weight.shape[0], 2, channels)
        return ordered(first_c, pick(parts, c, 1), swap(pick(parts, 1 - c, 1), "c"), 0)

    branch_shard, recur_in_shard = core_columns(w_branch), core_columns(w_recur_in)
    (
        branch_shard, recur_in_shard, w_recur_out, w_rgate, w_gate, w_up, w_down, norm_gain
    ) = lax.optimization_barrier(
        (branch_shard, recur_in_shard, w_recur_out, w_rgate, w_gate, w_up, w_down, norm_gain)
    )

    gains = jnp.stack([norm_gain, mlp_gain]).reshape(1, -1)
    gains = lax.all_to_all(jnp.tile(gains, (devices, 1)), EVERY, 0, 0, tiled=True)
    gains = jnp.swapaxes(gains.reshape(devices, 2, -1), 0, 1).reshape(2, width).astype(F32)
    ngain, mgain = gains[0], gains[1]

    vectors = jnp.concatenate(
        [conv_weight, conv_bias[None], rgate_bias[None], igate_bias[None], rate_param[None]]
    )
    vectors = jnp.pad(vectors.T, ((0, 0), (0, 120)))
    out_gates = jnp.concatenate([w_recur_out, w_rgate, w_igate, vectors], axis=1)
    out_gates = lax.all_gather(out_gates, EVERY, axis=0, tiled=True)
    out_gates = pick(out_gates.reshape(2, channels, -1), c, 0)
    out_full, gates = out_gates[:, :width], out_gates[:, width:]
    branch_full = fine_gather(z_gather(branch_shard), "y", "x")
    recur_in_full = fine_gather(z_gather(recur_in_shard), "x", "y")

    units = w_gate.shape[1] // 2
    gate_up = jnp.stack([w_gate, w_up], 1).reshape(w_gate.shape[0], 2, 2, units)
    mine = pick(gate_up, y, 2).reshape(-1, 2 * units)
    theirs = swap(pick(gate_up, 1 - y, 2).reshape(-1, 2 * units), "y")
    gate_up_shard = ordered(first_y, mine, theirs, 0)
    gate_up_full = lax.all_gather(gate_up_shard, "z", axis=0, tiled=True)
    down = w_down.reshape(2, units, -1)
    down_shard = ordered(first_y, pick(down, y, 0), swap(pick(down, 1 - y, 0), "y"), 1)

    vec = gates[:, 512:520].T.astype(F32)
    rate = vec[7]
    eight = -8.0 * jax.nn.softplus(rate)
    vec = jnp.concatenate([vec[:7], eight[None]])

    rows_in = own_sequence(block_input).astype(F32)
    normed_f, norm_pull = jax.vjp(rms_scale, rows_in, ngain)
    normed = fine_order(low(normed_f))
    normed = jnp.concatenate([normed, swap(normed, "c")])
    branch_pre = mm(normed, branch_full)
    recur_pre = mm(normed, recur_in_full).reshape(2, length, channels)
    branch_act, gelu_pull = jax.vjp(partial(jax.nn.gelu, approximate=True), branch_pre)
    halo = z_shift(recur_pre[:, length - 8 :], 1)
    conv, sig_r, sig_i, decay, state, prod = run_forward(recur_pre, halo, vec, gates)
    carry = z_carry(prod[:, -1], state[:, -1], 1)
    carry, down_shard = lax.optimization_barrier((carry, down_shard))
    down_across = lax.all_gather(down_shard.T, "z", axis=0, tiled=True)
    states = (state + prod * carry[:, None]).reshape(2 * length, channels)
    mixed_low = low(states * branch_act)
    recur_out = mm(mixed_low, out_full)
    middle = rows_in + recur_out[:length] + swap(recur_out[length:], "c")

    normed2_f, norm2_pull = jax.vjp(rms_scale, middle, mgain)
    tokens_all = group_gather(low(normed2_f))
    pre = mm(tokens_all, gate_up_full)
    hidden_f, mlp_pull = jax.vjp(mlp_act, pre[:, :units], pre[:, units:])
    hidden = low(hidden_f)
    mlp_out = group_scatter(mm_rows(hidden, down_across))
    block_output = own_tokens(low(middle + mlp_out))

    own_grad = own_sequence(cotangent)
    grad_all = group_gather(own_grad)
    grad_hidden = mm(grad_all, down_across)
    grad_pre = jnp.concatenate([low(g) for g in mlp_pull(grad_hidden)], axis=1)
    grad_normed2 = group_scatter(mm_rows(grad_pre, gate_up_full))
    block = width // z_count
    grad_gate_up = lax.psum_scatter(
        low(outer_sum(tokens_all, grad_pre)), "z", scatter_dimension=0, tiled=True
    ).astype(F32)
    grad_down = lax.psum_scatter(
        low(outer_sum(grad_all, hidden)), "z", scatter_dimension=0, tiled=True
    ).astype(F32)
    grad_gate_up = grad_gate_up.reshape(2, block // 2, 2 * units)
    gate_up_kept = pick(grad_gate_up, y, 0).reshape(-1, 2, 1, units)
    gate_up_other = swap(low(pick(grad_gate_up, 1 - y, 0)), "y")
    grad_down = grad_down.reshape(2, -1, units)
    down_kept, down_other = pick(grad_down, y, 0), swap(low(pick(grad_down, 1 - y, 0)), "y")

    grad_middle_norm, grad_mgain = norm2_pull(grad_normed2)
    grad_middle = own_grad.astype(F32) + grad_middle_norm
    grad_out_low = low(grad_middle)
    grad_out_low = jnp.concatenate([grad_out_low, swap(grad_out_low, "c")])
    grad_mixed = mm_rows(grad_out_low, out_full)
    grad_states = (grad_mixed * branch_act).reshape(2, length, channels)
    grad_branch_low = low(gelu_pull(grad_mixed * states)[0])

    def quarter(grad):
        def part(at):
            rows = lax.dynamic_slice_in_dim(normed, at * (width // 4), width // 4, 1)
            return outer_sum(rows, grad)

        return part

    block, corner, far, onward = fine_near(quarter(grad_branch_low), "y", "x")
    local, ahead, sent = run_reverse(decay, grad_states)
    entering = z_carry(prod[:, -1], sent, -1)
    entering, corner = lax.optimization_barrier((entering, corner))
    near = onward(corner)
    grad_conv, grad_rgate, grad_igate, small = run_backward(
        local, ahead, entering, state, prod, carry, conv, sig_r, sig_i, recur_pre, halo, vec, gates
    )

    rim = z_shift(grad_conv[:, :8], -1)
    grad_ext = jnp.concatenate([grad_conv, rim], axis=1)
    grad_recur_low = low(sum(vec[k] * grad_ext[:, k : k + length] for k in range(CONV)))
    grad_recur_low = grad_recur_low.reshape(2 * length, channels)
    grad_recur_low, far, near = lax.optimization_barrier((grad_recur_low, far, near))
    branch_near = fine_total(block, far, near)
    grad_normed = mm_rows(grad_branch_low, branch_full) + mm_rows(grad_recur_low, recur_in_full)
    grad_normed = grad_normed[:length] + swap(grad_normed[length:], "c")
    grad_rows, grad_ngain = norm_pull(fine_back(grad_normed))
    input_rows = low(grad_middle + grad_rows)

    def own_rows(chunk):
        parts = chunk.reshape(2, -1, channels)
        return ordered(first_c, pick(parts, c, 0), swap(pick(parts, 1 - c, 0), "c"), 1)

    from_halves = [(target, source) for source, target in to_halves(devices)]
    small = jnp.concatenate([small[:7], (small[7] * -8.0 * jax.nn.sigmoid(rate))[None]])
    small = jnp.pad(small.T, ((0, 0), (0, 120)))
    out_grads = [low(g) for g in (outer_sum(mixed_low, grad_out_low), grad_rgate, grad_igate, small)]
    out_grads = jnp.concatenate(out_grads, axis=1)
    out_grads = lax.psum_scatter(out_grads, CHIPS, scatter_dimension=0, tiled=True)
    out_grads = lax.ppermute(out_grads, EVERY, from_halves).astype(F32)
    grad_recur_out, gate_grads = out_grads[:, :width], out_grads[:, width:]
    small = gate_grads[:, 512:520].T
    grad_branch = own_rows(z_scatter(branch_near))
    block, corner, far, onward = fine_near(quarter(grad_recur_low), "x", "y")
    recur_in_near = fine_total(block, far, onward(corner))
    (
        recur_in_near, gate_up_other, down_other, grad_ngain, grad_mgain, input_rows
    ) = lax.optimization_barrier(
        (recur_in_near, gate_up_other, down_other, grad_ngain, grad_mgain, input_rows)
    )
    grad_recur_in = own_rows(z_scatter(recur_in_near))
    input_grad = own_tokens(input_rows)
    gate_up_other = gate_up_other.astype(F32).reshape(-1, 2, 1, units)
    both = ordered(first_y, gate_up_kept, gate_up_other, 2).reshape(-1, 2, 2 * units)
    grad_gate, grad_up = both[:, 0], both[:, 1]
    grad_down = ordered(first_y, down_kept, down_other.astype(F32), 1).T
    gain_grads = jnp.stack([grad_ngain, grad_mgain])
    for axis in ("c", "x", "y"):
        gain_grads = gain_grads + swap(gain_grads, axis)
    if z_direct():
        gain_grads = gain_grads + sum(z_send(gain_grads, j) for j in range(1, z_count))
    else:
        gain_grads = lax.psum(gain_grads, "z")
    gain_grads = pick(gain_grads.reshape(2, devices, -1), lax.axis_index(EVERY), 1)
    return (
        block_output,
        input_grad,
        grad_branch,
        grad_recur_in,
        grad_recur_out,
        gate_grads[:, :256],
        gate_grads[:, 256:512],
        small[:4],
        small[4],
        small[5],
        small[6],
        small[7],
        gain_grads[0],
        gain_grads[1],
        grad_gate,
        grad_up,
        grad_down,
    )


def solution(mesh):
    seq, mlp = mesh.shape["seq"], mesh.shape["mlp"]
    fine = Mesh(mesh.devices.reshape(seq // 2, 2, mlp // 2, 2), EVERY)
    over_seq, over_mlp = ("z", "y"), ("x", "c")
    rows, channel, vector = P(EVERY, None), P(None, EVERY), P(EVERY)
    tokens = P(over_mlp, over_seq, None)
    in_specs = (
        (tokens,) + (rows,) * 5 + (channel,) + (vector,) * 6
        + (P(over_seq, over_mlp), P(over_seq, over_mlp), P(over_mlp, over_seq), tokens)
    )
    out_specs = (
        (tokens, tokens) + (rows,) * 5 + (channel,) + (vector,) * 6
        + (P(over_seq, over_mlp), P(over_seq, over_mlp), P(over_mlp, over_seq))
    )
    return jax.shard_map(
        on_device, mesh=fine, in_specs=in_specs, out_specs=out_specs, check_vma=False
    )
```

```python
from functools import partial

import jax
import jax.numpy as jnp
from jax import lax
from jax.experimental import pallas as pl
from jax.experimental.pallas import tpu as pltpu
from jax.sharding import Mesh, PartitionSpec as P

HEADS = 10
CONV = 4
F32 = jnp.float32
BF16 = jnp.bfloat16
PAIR = ((0, 1), (1, 0))


def swap(value, axis):
    return lax.ppermute(value, axis, PAIR)


def low(value):
    return value.astype(BF16)


def ordered(first, mine, theirs, axis):
    return jnp.where(
        first, jnp.concatenate([mine, theirs], axis), jnp.concatenate([theirs, mine], axis)
    )


def pick(array, index, axis):
    return lax.dynamic_index_in_dim(array, index, axis, keepdims=False)


def z_direct():
    return lax.axis_size("z") == 4


def z_send(value, j):
    count = lax.axis_size("z")
    return lax.ppermute(value, "z", [(s, s ^ j) for s in range(count)])


def place(pieces, size):
    rows = pieces[0][1].shape[0]
    full = jnp.zeros((size * rows,) + pieces[0][1].shape[1:], pieces[0][1].dtype)
    for at, piece in pieces:
        full = lax.dynamic_update_slice_in_dim(full, piece, at * rows, 0)
    return full


def z_gather(shard):
    count = lax.axis_size("z")
    if not z_direct():
        return lax.all_gather(shard, "z", axis=0, tiled=True)
    z = lax.axis_index("z")
    pieces = [(z, shard)] + [(z ^ j, z_send(shard, j)) for j in range(1, count)]
    return place(pieces, count)


def z_scatter(part):
    count = lax.axis_size("z")
    if not z_direct():
        return lax.psum_scatter(low(part), "z", scatter_dimension=0, tiled=True).astype(F32)
    z, rows = lax.axis_index("z"), part.shape[0] // count
    total = lax.dynamic_slice_in_dim(part, z * rows, rows, 0)
    for j in range(1, count):
        block = lax.dynamic_slice_in_dim(part, (z ^ j) * rows, rows, 0)
        total = total + z_send(low(block), j).astype(F32)
    return total


def z_shift(value, steps):
    count = lax.axis_size("z")
    return lax.ppermute(
        value, "z", [(s, s + steps) for s in range(count) if 0 <= s + steps < count]
    )


def z_carry(decay, state, step):
    count = lax.axis_size("z")
    pair = jnp.stack([decay, state])
    if z_direct():
        near = [z_shift(pair, step * k) for k in range(1, count)]
        carry = near[-1][1]
        for got in near[-2::-1]:
            carry = got[1] + got[0] * carry
        return carry
    everything, here = lax.all_gather(pair, "z"), lax.axis_index("z")

    def hop(k, before):
        at = k if step == 1 else count - 1 - k
        reached = at < here if step == 1 else at > here
        return jnp.where(reached, everything[at, 1] + everything[at, 0] * before, before)

    return lax.fori_loop(0, count, hop, jnp.zeros_like(state))


def group_gather(own):
    half = own.shape[0] // 2
    over_x, over_y = swap(own, "x"), swap(own, "y")
    corner = jnp.concatenate([swap(over_x[:half], "y"), swap(over_y[half:], "x")])
    near = jnp.concatenate([over_x, over_y, corner])
    return jnp.concatenate([own, near, swap(own, "c"), swap(near, "c")])


def group_scatter(partial_sum):
    rows = partial_sum.shape[0] // 8
    mine = partial_sum[: 4 * rows] + swap(low(partial_sum[4 * rows :]), "c").astype(F32)
    own, to_x, to_y, corner = (mine[k * rows : (k + 1) * rows] for k in range(4))
    half = rows // 2
    via_x = swap(low(corner[:half]), "x").astype(F32)
    via_y = swap(low(corner[half:]), "y").astype(F32)
    to_y = jnp.concatenate([to_y[:half] + via_x, to_y[half:]])
    to_x = jnp.concatenate([to_x[:half], to_x[half:] + via_y])
    return own + swap(low(to_x), "x").astype(F32) + swap(low(to_y), "y").astype(F32)


def fine_order(values):
    count = lax.axis_size("z")
    blocks = values.reshape(values.shape[0], count, 2, 2, -1)
    return jnp.transpose(blocks, (0, 3, 2, 1, 4)).reshape(values.shape)


def fine_back(values):
    count = lax.axis_size("z")
    blocks = values.reshape(values.shape[0], 2, 2, count, -1)
    return jnp.transpose(blocks, (0, 3, 2, 1, 4)).reshape(values.shape)


def fine_gather(own, first, second):
    x, y = lax.axis_index("x"), lax.axis_index("y")
    far = swap(own, second)
    near = swap(own, first)
    both = swap(near, second)
    over_y, over_x = (near, far) if first == "y" else (far, near)
    return place(
        [
            (2 * x + y, own),
            (2 * x + (1 - y), over_y),
            (2 * (1 - x) + y, over_x),
            (2 * (1 - x) + (1 - y), both),
        ],
        4,
    )


def fine_near(part, first, second):
    x, y = lax.axis_index("x"), lax.axis_index("y")

    def block(on_first, on_second):
        over_x, over_y = (on_second, on_first) if second == "x" else (on_first, on_second)
        return part(2 * (x ^ over_x) + (y ^ over_y))

    corner = swap(low(block(1, 1)), second)
    far = swap(low(block(0, 1)), second)
    return block, corner, far, lambda got: swap(low(block(1, 0) + got.astype(F32)), first)


def fine_total(block, far, near):
    return block(0, 0) + far.astype(F32) + near.astype(F32)


def to_halves(count):
    return [(count // 2 * c + q, 2 * q + c) for q in range(count // 2) for c in range(2)]


EVERY = ("z", "y", "x", "c")
CHIPS = ("z", "y", "x")


def expm1_neg(value):
    series = 1.0
    for k in range(10, 1, -1):
        series = 1.0 + value / k * series
    return jnp.where(value > -1.0, -value * series, 1.0 - jnp.exp(value))


def forward_kernel(
    rec_ref, halo_ref, vec_ref, wr_ref, wi_ref, conv_ref, sr_ref, si_ref, a_ref, s_ref, p_ref, ext
):
    head, heads = pl.program_id(0), pl.num_programs(0)
    seqs, length, width = rec_ref.shape
    lanes = pl.ds(pl.multiple_of(head * width, width), width)
    vec = vec_ref[...]
    for s in range(seqs):
        ext[s, 0:8, :] = halo_ref[s]
        ext[s, 8 : 8 + length, :] = rec_ref[s]
        conv = vec[4:5] + sum(
            vec[k : k + 1] * ext[s, 8 - k : 8 - k + length, :] for k in range(CONV)
        )
        conv_low = low(conv)
        sig_r = jax.nn.sigmoid(
            jnp.dot(conv_low, wr_ref[...], preferred_element_type=F32) + vec[5:6]
        )
        sig_i = jax.nn.sigmoid(
            jnp.dot(conv_low, wi_ref[...], preferred_element_type=F32) + vec[6:7]
        )
        decay_log = vec[7:8] * sig_r
        conv_ref[s] = conv
        sr_ref[s] = sig_r
        si_ref[s] = sig_i
        a_ref[s, :, lanes] = jnp.exp(decay_log)
        s_ref[s, :, lanes] = sig_i * conv * jnp.sqrt(expm1_neg(2.0 * decay_log))

    @pl.when(head == heads - 1)
    def _():
        def step(t, carry):
            new = []
            for s in range(seqs):
                prod, state = carry[s]
                row = pl.ds(t, 1)
                decay = a_ref[s, row, :]
                prod = decay * prod
                state = decay * state + s_ref[s, row, :]
                p_ref[s, row, :] = prod
                s_ref[s, row, :] = state
                new.append((prod, state))
            return tuple(new)

        full = a_ref.shape[2]
        start = (jnp.ones((1, full), F32), jnp.zeros((1, full), F32))
        lax.fori_loop(0, length, step, (start,) * seqs)


def reverse_kernel(a_ref, g_ref, l_ref, q_ref, e_ref):
    seqs, length, full = a_ref.shape

    def step(k, carry):
        t = length - 1 - k
        new = []
        for s in range(seqs):
            prod, sent = carry[s]
            row = pl.ds(t, 1)
            q_ref[s, row, :] = prod
            delta = g_ref[s, row, :] + sent
            l_ref[s, row, :] = delta
            decay = a_ref[s, row, :]
            new.append((prod * decay, decay * delta))
        return tuple(new)

    start = (jnp.ones((1, full), F32), jnp.zeros((1, full), F32))
    last = lax.fori_loop(0, length, step, (start,) * seqs)
    for s in range(seqs):
        e_ref[pl.ds(s, 1), :] = last[s][1]


def backward_kernel(
    l_ref, q_ref, e_ref, s_ref, p_ref, carry_ref, conv_ref, sr_ref, si_ref, rec_ref, halo_ref,
    vec_ref, wr_ref, wi_ref, gconv_ref, gwr_ref, gwi_ref, small_ref, ext, before,
):
    seqs, length, width = rec_ref.shape
    vec = vec_ref[...]
    rows = [jnp.zeros((1, width), F32)] * 8
    contract_rows = (((0,), (0,)), ((), ()))
    contract_last = (((1,), (1,)), ((), ()))
    for s in range(seqs):
        ext[s, 0:8, :] = halo_ref[s]
        ext[s, 8 : 8 + length, :] = rec_ref[s]
        carry = carry_ref[s : s + 1, :]
        before[s, 0:8, :] = jnp.broadcast_to(carry, (8, width))
        before[s, 8 : 8 + length, :] = s_ref[s] + p_ref[s] * carry
        prev = before[s, 7 : 7 + length, :]
        delta = l_ref[s] + q_ref[s] * e_ref[s : s + 1, :]
        conv, sig_r, sig_i = conv_ref[s], sr_ref[s], si_ref[s]
        decay_log = vec[7:8] * sig_r
        decay = jnp.exp(decay_log)
        scale = jnp.sqrt(expm1_neg(2.0 * decay_log))
        through = delta * sig_i
        grad_log = delta * prev * decay - through * conv * decay * decay / scale
        slope_r = grad_log * sig_r
        rows[7] = rows[7] + jnp.sum(slope_r, axis=0, keepdims=True)
        grad_r = low(slope_r * vec[7:8] * (1.0 - sig_r))
        grad_i = low(through * conv * scale * (1.0 - sig_i))
        conv_low = low(conv)
        gwr = lax.dot_general(conv_low, grad_r, contract_rows, preferred_element_type=F32)
        gwi = lax.dot_general(conv_low, grad_i, contract_rows, preferred_element_type=F32)
        if s == 0:
            gwr_ref[...], gwi_ref[...] = gwr, gwi
        else:
            gwr_ref[...] += gwr
            gwi_ref[...] += gwi
        rows[5] = rows[5] + jnp.sum(grad_r.astype(F32), axis=0, keepdims=True)
        rows[6] = rows[6] + jnp.sum(grad_i.astype(F32), axis=0, keepdims=True)
        grad_conv = (
            through * scale
            + lax.dot_general(grad_r, wr_ref[...], contract_last, preferred_element_type=F32)
            + lax.dot_general(grad_i, wi_ref[...], contract_last, preferred_element_type=F32)
        )
        gconv_ref[s] = grad_conv
        rows[4] = rows[4] + jnp.sum(grad_conv, axis=0, keepdims=True)
        for k in range(CONV):
            tap = grad_conv * ext[s, 8 - k : 8 - k + length, :]
            rows[k] = rows[k] + jnp.sum(tap, axis=0, keepdims=True)
    for k in range(8):
        small_ref[k : k + 1, :] = rows[k]


def cost(flops, values):
    return pl.CostEstimate(flops=flops, bytes_accessed=values, transcendentals=0)


def run_forward(rec, halo, vec, gates):
    seqs, length, full = rec.shape
    heads = HEADS // 2
    width = full // heads
    block = pl.BlockSpec((seqs, length, width), lambda h: (0, 0, h))
    whole = pl.BlockSpec((seqs, length, full), lambda h: (0, 0, 0))
    array = jax.ShapeDtypeStruct(rec.shape, F32)
    return pl.pallas_call(
        forward_kernel,
        grid=(heads,),
        in_specs=[
            block,
            pl.BlockSpec((seqs, 8, width), lambda h: (0, 0, h)),
            pl.BlockSpec((8, width), lambda h: (0, h)),
            pl.BlockSpec((width, width), lambda h: (h, 0)),
            pl.BlockSpec((width, width), lambda h: (h, 1)),
        ],
        out_specs=[block, block, block, whole, whole, whole],
        out_shape=[array] * 6,
        scratch_shapes=[pltpu.VMEM((seqs, length + 8, width), F32)],
        cost_estimate=cost(seqs * length * full * width * 4, rec.size * 28),
        name="recur_forward",
    )(rec, halo, vec, gates, gates)


def run_reverse(decay, grad_states):
    seqs, length, full = decay.shape
    array = jax.ShapeDtypeStruct(decay.shape, F32)
    return pl.pallas_call(
        reverse_kernel,
        out_shape=[array, array, jax.ShapeDtypeStruct((seqs, full), F32)],
        cost_estimate=cost(decay.size * 4, decay.size * 16),
        name="recur_reverse",
    )(decay, grad_states)


def run_backward(local, ahead, entering, state, prod, carry, conv, sig_r, sig_i, rec, halo, vec, gates):
    seqs, length, full = rec.shape
    heads = HEADS // 2
    width = full // heads
    block = pl.BlockSpec((seqs, length, width), lambda h: (0, 0, h))
    row = pl.BlockSpec((seqs, width), lambda h: (0, h))
    weight = pl.BlockSpec((width, width), lambda h: (h, 0))
    return pl.pallas_call(
        backward_kernel,
        grid=(heads,),
        in_specs=[
            block,
            block,
            row,
            block,
            block,
            row,
            block,
            block,
            block,
            block,
            pl.BlockSpec((seqs, 8, width), lambda h: (0, 0, h)),
            pl.BlockSpec((8, width), lambda h: (0, h)),
            pl.BlockSpec((width, width), lambda h: (h, 0)),
            pl.BlockSpec((width, width), lambda h: (h, 1)),
        ],
        out_specs=[block, weight, weight, pl.BlockSpec((8, width), lambda h: (0, h))],
        out_shape=[
            jax.ShapeDtypeStruct(rec.shape, F32),
            jax.ShapeDtypeStruct((full, width), F32),
            jax.ShapeDtypeStruct((full, width), F32),
            jax.ShapeDtypeStruct((8, full), F32),
        ],
        scratch_shapes=[pltpu.VMEM((seqs, length + 8, width), F32)] * 2,
        cost_estimate=cost(seqs * length * full * width * 8, rec.size * 40),
        name="recur_backward",
    )(local, ahead, entering, state, prod, carry, conv, sig_r, sig_i, rec, halo, vec, gates, gates)


def rms_scale(values, gain):
    return values * lax.rsqrt(jnp.mean(values * values, axis=-1, keepdims=True) + 1e-06) * gain


def mlp_act(gate_pre, up_pre):
    return jax.nn.gelu(gate_pre, approximate=True) * up_pre


def mm(left, right):
    return jnp.dot(left, right, preferred_element_type=F32)


def mm_rows(left, weight):
    return lax.dot_general(left, weight, (((1,), (1,)), ((), ())), preferred_element_type=F32)


def outer_sum(left, right):
    return lax.dot_general(left, right, (((0,), (0,)), ((), ())), preferred_element_type=F32)


def on_device(
    block_input,
    w_branch,
    w_recur_in,
    w_recur_out,
    w_rgate,
    w_igate,
    conv_weight,
    conv_bias,
    rgate_bias,
    igate_bias,
    rate_param,
    norm_gain,
    mlp_gain,
    w_gate,
    w_up,
    w_down,
    cotangent,
):
    z, y, c = (lax.axis_index(axis) for axis in ("z", "y", "c"))
    z_count = lax.axis_size("z")
    devices = z_count * 8
    first_y, first_c = y == 0, c == 0
    half_tokens, width = block_input.shape[1:]
    length = 2 * half_tokens
    channels = w_branch.shape[1] // 2

    def own_sequence(block):
        return ordered(first_y, pick(block, y, 0), swap(pick(block, 1 - y, 0), "y"), 0)

    def own_tokens(rows):
        halves = rows.reshape(2, half_tokens, width)
        mine, theirs = pick(halves, y, 0), swap(pick(halves, 1 - y, 0), "y")
        return jnp.where(first_y, jnp.stack([mine, theirs]), jnp.stack([theirs, mine]))

    def core_columns(weight):
        parts = weight.reshape(weight.shape[0], 2, channels)
        return ordered(first_c, pick(parts, c, 1), swap(pick(parts, 1 - c, 1), "c"), 0)

    branch_shard, recur_in_shard = core_columns(w_branch), core_columns(w_recur_in)
    (
        branch_shard, recur_in_shard, w_recur_out, w_rgate, w_gate, w_up, w_down, norm_gain
    ) = lax.optimization_barrier(
        (branch_shard, recur_in_shard, w_recur_out, w_rgate, w_gate, w_up, w_down, norm_gain)
    )

    vectors = jnp.concatenate(
        [conv_weight, conv_bias[None], rgate_bias[None], igate_bias[None], rate_param[None]]
    )
    gains = jnp.concatenate([norm_gain, mlp_gain, vectors.reshape(-1)]).reshape(1, -1)
    gains = lax.all_to_all(jnp.tile(gains, (devices, 1)), EVERY, 0, 0, tiled=True)
    gains, vectors = gains[:, : 2 * norm_gain.shape[0]], gains[:, 2 * norm_gain.shape[0] :]
    gains = jnp.swapaxes(gains.reshape(devices, 2, -1), 0, 1).reshape(2, width).astype(F32)
    ngain, mgain = gains[0], gains[1]
    vectors = jnp.swapaxes(vectors.reshape(devices, 8, -1), 0, 1).reshape(8, 2, channels)

    out_gates = jnp.concatenate([w_recur_out, w_rgate, w_igate], axis=1)
    out_gates = lax.all_gather(out_gates, EVERY, axis=0, tiled=True)
    out_gates = pick(out_gates.reshape(2, channels, -1), c, 0)
    out_full, gates = out_gates[:, :width], out_gates[:, width:]
    branch_full = fine_gather(z_gather(branch_shard), "y", "x")
    recur_in_full = fine_gather(z_gather(recur_in_shard), "x", "y")

    units = w_gate.shape[1] // 2
    gate_up = jnp.stack([w_gate, w_up], 1).reshape(w_gate.shape[0], 2, 2, units)
    mine = pick(gate_up, y, 2).reshape(-1, 2 * units)
    theirs = swap(pick(gate_up, 1 - y, 2).reshape(-1, 2 * units), "y")
    gate_up_shard = ordered(first_y, mine, theirs, 0)
    gate_up_full = lax.all_gather(gate_up_shard, "z", axis=0, tiled=True)
    down = w_down.reshape(2, units, -1)
    down_shard = ordered(first_y, pick(down, y, 0), swap(pick(down, 1 - y, 0), "y"), 1)

    vec = pick(vectors, c, 1).astype(F32)
    rate = vec[7]
    eight = -8.0 * jax.nn.softplus(rate)
    vec = jnp.concatenate([vec[:7], eight[None]])

    rows_in = own_sequence(block_input).astype(F32)
    normed_f, norm_pull = jax.vjp(rms_scale, rows_in, ngain)
    normed = fine_order(low(normed_f))
    normed = jnp.concatenate([normed, swap(normed, "c")])
    branch_pre = mm(normed, branch_full)
    recur_pre = mm(normed, recur_in_full).reshape(2, length, channels)
    branch_act, gelu_pull = jax.vjp(partial(jax.nn.gelu, approximate=True), branch_pre)
    halo = z_shift(recur_pre[:, length - 8 :], 1)
    conv, sig_r, sig_i, decay, state, prod = run_forward(recur_pre, halo, vec, gates)
    carry = z_carry(prod[:, -1], state[:, -1], 1)
    carry, down_shard = lax.optimization_barrier((carry, down_shard))
    down_across = lax.all_gather(down_shard.T, "z", axis=0, tiled=True)
    states = (state + prod * carry[:, None]).reshape(2 * length, channels)
    mixed_low = low(states * branch_act)
    recur_out = mm(mixed_low, out_full)
    middle = rows_in + recur_out[:length] + swap(recur_out[length:], "c")

    normed2_f, norm2_pull = jax.vjp(rms_scale, middle, mgain)
    tokens_all = group_gather(low(normed2_f))
    pre = mm(tokens_all, gate_up_full)
    hidden_f, mlp_pull = jax.vjp(mlp_act, pre[:, :units], pre[:, units:])
    hidden = low(hidden_f)
    mlp_out = group_scatter(mm_rows(hidden, down_across))
    block_output = own_tokens(low(middle + mlp_out))

    own_grad = own_sequence(cotangent)
    grad_all = group_gather(own_grad)
    grad_hidden = mm(grad_all, down_across)
    grad_pre = jnp.concatenate([low(g) for g in mlp_pull(grad_hidden)], axis=1)
    grad_normed2 = group_scatter(mm_rows(grad_pre, gate_up_full))
    block = width // z_count
    grad_gate_up = lax.psum_scatter(
        low(outer_sum(tokens_all, grad_pre)), "z", scatter_dimension=0, tiled=True
    ).astype(F32)
    grad_down = lax.psum_scatter(
        low(outer_sum(grad_all, hidden)), "z", scatter_dimension=0, tiled=True
    ).astype(F32)
    grad_gate_up = grad_gate_up.reshape(2, block // 2, 2 * units)
    gate_up_kept = pick(grad_gate_up, y, 0).reshape(-1, 2, 1, units)
    gate_up_other = swap(low(pick(grad_gate_up, 1 - y, 0)), "y")
    grad_down = grad_down.reshape(2, -1, units)
    down_kept, down_other = pick(grad_down, y, 0), swap(low(pick(grad_down, 1 - y, 0)), "y")

    grad_middle_norm, grad_mgain = norm2_pull(grad_normed2)
    grad_middle = own_grad.astype(F32) + grad_middle_norm
    grad_out_low = low(grad_middle)
    grad_out_low = jnp.concatenate([grad_out_low, swap(grad_out_low, "c")])
    grad_mixed = mm_rows(grad_out_low, out_full)
    grad_states = (grad_mixed * branch_act).reshape(2, length, channels)
    grad_branch_low = low(gelu_pull(grad_mixed * states)[0])

    def quarter(grad):
        def part(at):
            rows = lax.dynamic_slice_in_dim(normed, at * (width // 4), width // 4, 1)
            return outer_sum(rows, grad)

        return part

    block, corner, far, onward = fine_near(quarter(grad_branch_low), "y", "x")
    local, ahead, sent = run_reverse(decay, grad_states)
    entering = z_carry(prod[:, -1], sent, -1)
    entering, corner = lax.optimization_barrier((entering, corner))
    near = onward(corner)
    grad_conv, grad_rgate, grad_igate, small = run_backward(
        local, ahead, entering, state, prod, carry, conv, sig_r, sig_i, recur_pre, halo, vec, gates
    )

    rim = z_shift(grad_conv[:, :8], -1)
    grad_ext = jnp.concatenate([grad_conv, rim], axis=1)
    grad_recur_low = low(sum(vec[k] * grad_ext[:, k : k + length] for k in range(CONV)))
    grad_recur_low = grad_recur_low.reshape(2 * length, channels)
    grad_recur_low, far, near = lax.optimization_barrier((grad_recur_low, far, near))
    branch_near = fine_total(block, far, near)
    grad_normed = mm_rows(grad_branch_low, branch_full) + mm_rows(grad_recur_low, recur_in_full)
    grad_normed = grad_normed[:length] + swap(grad_normed[length:], "c")
    grad_rows, grad_ngain = norm_pull(fine_back(grad_normed))
    input_rows = low(grad_middle + grad_rows)

    def own_rows(chunk):
        parts = chunk.reshape(2, -1, channels)
        return ordered(first_c, pick(parts, c, 0), swap(pick(parts, 1 - c, 0), "c"), 1)

    from_halves = [(target, source) for source, target in to_halves(devices)]
    small = jnp.concatenate([small[:7], (small[7] * -8.0 * jax.nn.sigmoid(rate))[None]])
    small = jnp.pad(small.T, ((0, 0), (0, 120)))
    out_grads = [low(g) for g in (outer_sum(mixed_low, grad_out_low), grad_rgate, grad_igate, small)]
    out_grads = jnp.concatenate(out_grads, axis=1)
    out_grads = lax.psum_scatter(out_grads, CHIPS, scatter_dimension=0, tiled=True)
    out_grads = lax.ppermute(out_grads, EVERY, from_halves).astype(F32)
    grad_recur_out, gate_grads = out_grads[:, :width], out_grads[:, width:]
    small = gate_grads[:, 512:520].T
    grad_branch = own_rows(z_scatter(branch_near))
    block, corner, far, onward = fine_near(quarter(grad_recur_low), "x", "y")
    recur_in_near = fine_total(block, far, onward(corner))
    (
        recur_in_near, gate_up_other, down_other, grad_ngain, grad_mgain, input_rows
    ) = lax.optimization_barrier(
        (recur_in_near, gate_up_other, down_other, grad_ngain, grad_mgain, input_rows)
    )
    grad_recur_in = own_rows(z_scatter(recur_in_near))
    input_grad = own_tokens(input_rows)
    gate_up_other = gate_up_other.astype(F32).reshape(-1, 2, 1, units)
    both = ordered(first_y, gate_up_kept, gate_up_other, 2).reshape(-1, 2, 2 * units)
    grad_gate, grad_up = both[:, 0], both[:, 1]
    grad_down = ordered(first_y, down_kept, down_other.astype(F32), 1).T
    gain_grads = jnp.stack([grad_ngain, grad_mgain])
    for axis in ("c", "x", "y"):
        gain_grads = gain_grads + swap(gain_grads, axis)
    if z_direct():
        gain_grads = gain_grads + sum(z_send(gain_grads, j) for j in range(1, z_count))
    else:
        gain_grads = lax.psum(gain_grads, "z")
    gain_grads = pick(gain_grads.reshape(2, devices, -1), lax.axis_index(EVERY), 1)
    return (
        block_output,
        input_grad,
        grad_branch,
        grad_recur_in,
        grad_recur_out,
        gate_grads[:, :256],
        gate_grads[:, 256:512],
        small[:4],
        small[4],
        small[5],
        small[6],
        small[7],
        gain_grads[0],
        gain_grads[1],
        grad_gate,
        grad_up,
        grad_down,
    )


def solution(mesh):
    seq, mlp = mesh.shape["seq"], mesh.shape["mlp"]
    fine = Mesh(mesh.devices.reshape(seq // 2, 2, mlp // 2, 2), EVERY)
    over_seq, over_mlp = ("z", "y"), ("x", "c")
    rows, channel, vector = P(EVERY, None), P(None, EVERY), P(EVERY)
    tokens = P(over_mlp, over_seq, None)
    in_specs = (
        (tokens,) + (rows,) * 5 + (channel,) + (vector,) * 6
        + (P(over_seq, over_mlp), P(over_seq, over_mlp), P(over_mlp, over_seq), tokens)
    )
    out_specs = (
        (tokens, tokens) + (rows,) * 5 + (channel,) + (vector,) * 6
        + (P(over_seq, over_mlp), P(over_seq, over_mlp), P(over_mlp, over_seq))
    )
    return jax.shard_map(
        on_device, mesh=fine, in_specs=in_specs, out_specs=out_specs, check_vma=False
    )
```
